256 devices in a mesh: grp: 8 (over z), row: 32 (over x, y, core).
Axes of the slice: x: 4, y: 4, z: 8, core: 2. Of those that a mesh axis runs over, the one named last changes fastest.
Arguments:
- basis: float32 [65536, 1024], P(('grp', 'row')), may hold values from -40 to 40
- block: float32 [65536, 512], P(('grp', 'row')), may hold values from -600 to 600
- counts: int32 [8, 32], P('grp', 'row'), may hold values from 128 to 256, as said below
Outputs:
- new_block: float32 [65536, 512], P(('grp', 'row'))
- factor: float32 [512, 512], replicated
The draws below stay inside these ranges and needn't reach their ends.
Inputs may be any that keep to these rules, and one draw needn't show every extreme that they name: `counts`: each device's live rows are a multiple of 128, at most 256; one device holds exactly 256.
All inputs are finite; a program needn't handle non-finite values.
Results may differ from the reference program's by a relative error of at most 0.0003.
Values sent between devices are 32-bit elements; how exact they have to be, the bound alone decides.
No kernel may reach another device: no remote copies, remote signals or barrier semaphores. Data moves between devices by JAX's collectives and lax.ppermute only.
A program may use at most 64 MiB of HBM per device.

```python
import math
import jax
import jax.numpy as jnp
from jax import lax

M = 1024
K = 512
CAP = 256
ROWS_ALL = 65536
N_GRP = 8
N_ROW = 32


def draw_counts(key, part):
    tiles = CAP // 128
    upper = max(2, 2 * tiles // 3)
    base = jax.random.randint(key, (N_GRP * N_ROW,), 1, upper)
    heavy = jax.random.randint(jax.random.fold_in(key, 7), (), 0, N_GRP * N_ROW)
    places = jnp.arange(N_GRP * N_ROW, dtype=jnp.int32)
    filled = jnp.where(places == heavy, tiles, base)
    return (filled * 128).reshape(N_GRP, N_ROW).astype(jnp.int32)


def live_rows(key, part):
    filled = draw_counts(key, part).reshape(-1)
    positions = jnp.arange(ROWS_ALL, dtype=jnp.int32)
    limit = filled[positions // CAP]
    return (positions % CAP < limit).astype(jnp.float32)[:, None]


def basis_span(key, part):
    live = live_rows(key, part)
    raw = jax.random.normal(jax.random.fold_in(key, 101), (ROWS_ALL, M), jnp.float32) * live
    orthonormal, upper_part = jnp.linalg.qr(raw)
    orthonormal = orthonormal * live * math.sqrt(ROWS_ALL)
    tilt = jnp.eye(M, dtype=jnp.float32) + 0.032 * jax.random.normal(jax.random.fold_in(key, 102), (M, M), jnp.float32) / math.sqrt(M)
    spanned = jnp.dot(orthonormal, tilt, precision=lax.Precision.HIGHEST) * live
    return (spanned, live)


def draw_basis(key, part):
    spanned, live = basis_span(key, part)
    filler = 1.7 * jax.random.normal(jax.random.fold_in(key, 103), (ROWS_ALL, M), jnp.float32)
    return jnp.clip(spanned + (1.0 - live) * filler, -40.0, 40.0)


def draw_block(key, part):
    spanned, live = basis_span(key, part)
    amounts = 30.0 * jax.random.normal(jax.random.fold_in(key, 201), (M, K), jnp.float32) / math.sqrt(M)
    along = jnp.dot(spanned, amounts, precision=lax.Precision.HIGHEST)
    rough = jax.random.normal(jax.random.fold_in(key, 202), (ROWS_ALL, K), jnp.float32)
    column_scale = jnp.exp(jax.random.uniform(jax.random.fold_in(key, 203), (K,), jnp.float32, math.log(0.5), math.log(5.0)))
    mixing = jnp.eye(K, dtype=jnp.float32) + 0.3 * jax.random.normal(jax.random.fold_in(key, 204), (K, K), jnp.float32) / math.sqrt(K)
    off_span = jnp.dot(rough * column_scale[None, :], mixing, precision=lax.Precision.HIGHEST)
    filler = jax.random.normal(jax.random.fold_in(key, 205), (ROWS_ALL, K), jnp.float32)
    return jnp.clip(live * (along + off_span) + (1.0 - live) * filler, -600.0, 600.0)


def setup_inputs(seed: int = 0) -> dict:
    seeds = jax.random.split(jax.random.key(seed), 4)
    return {
        "basis": draw_basis(jax.random.fold_in(seeds[3], 71), 0),
        "block": draw_block(jax.random.fold_in(seeds[3], 71), 0),
        "counts": draw_counts(jax.random.fold_in(seeds[3], 71), 0),
    }


def reference(basis, block, counts):
    total = basis.shape[0]
    positions = jnp.arange(total, dtype=jnp.int32)
    owner = positions // CAP
    limit = counts.reshape(-1).astype(jnp.int32)[owner]
    live = (positions % CAP < limit).astype(basis.dtype)[:, None]
    basis_live = basis * live
    block_live = block * live
    coeffs = jnp.dot(basis_live.T, block_live, precision=lax.Precision.HIGHEST) / ROWS_ALL
    first_pass = block_live - jnp.dot(basis_live, coeffs, precision=lax.Precision.HIGHEST)
    correction = jnp.dot(basis_live.T, first_pass, precision=lax.Precision.HIGHEST) / ROWS_ALL
    residual = first_pass - jnp.dot(basis_live, correction, precision=lax.Precision.HIGHEST)
    gram = jnp.dot(residual.T, residual, precision=lax.Precision.HIGHEST) / ROWS_ALL
    lower_factor = jnp.linalg.cholesky(gram)
    new_block = lax.linalg.triangular_solve(lower_factor, residual, left_side=False, lower=True, transpose_a=True)
    return (new_block, lower_factor.T)
```

```python
import functools

import jax
import jax.numpy as jnp
from jax import lax
from jax.experimental import pallas as pl
from jax.experimental.pallas import tpu as pltpu
from jax.sharding import Mesh
from jax.sharding import PartitionSpec as P

ROW = ("row_0", "row_1", "row_2")
GRP_ROW = ("grp", "row_0", "row_1", "row_2")
PLANE = ("row_0", "row_1")

BLOCK = 128
PANEL = 8
HIGHEST = lax.Precision.HIGHEST


def dot_tn(a, b):
    return lax.dot_general(
        a, b, (((0,), (0,)), ((), ())), precision=HIGHEST, preferred_element_type=jnp.float32
    )


def dot_nn(a, b):
    return jnp.dot(a, b, precision=HIGHEST, preferred_element_type=jnp.float32)


def dot_nt(a, b):
    return lax.dot_general(
        a, b, (((1,), (1,)), ((), ())), precision=HIGHEST, preferred_element_type=jnp.float32
    )


def identity(n):
    return (
        lax.broadcasted_iota(jnp.int32, (n, n), 0) == lax.broadcasted_iota(jnp.int32, (n, n), 1)
    ).astype(jnp.float32)


def eliminate_block(d):
    n = BLOCK
    for b in range(0, n, PANEL):
        ra = [d[b + i : b + i + 1, 0:n] for i in range(PANEL)]
        re = [d[b + i : b + i + 1, n : 2 * n] for i in range(PANEL)]
        s = {}
        for i in range(PANEL):
            for j in range(i, PANEL):
                s[i, j] = jnp.broadcast_to(ra[i][:, b + j : b + j + 1], (1, n))
        for k in range(PANEL):
            inv = lax.rsqrt(s[k, k])
            ra[k] = ra[k] * inv
            re[k] = re[k] * inv
            r = [s[k, j] * inv if j > k else None for j in range(PANEL)]
            for i in range(k + 1, PANEL):
                for j in range(i, PANEL):
                    s[i, j] = s[i, j] - r[i] * r[j]
                ra[i] = ra[i] - r[i] * ra[k]
                re[i] = re[i] - r[i] * re[k]
            d[b + k : b + k + 1, 0:n] = ra[k]
            d[b + k : b + k + 1, n : 2 * n] = re[k]
        nxt = b + PANEL
        if nxt >= n:
            continue
        for i in range(PANEL):
            row = slice(nxt + i, nxt + i + 1)
            na, ne = d[row, 0:n], d[row, n : 2 * n]
            for k in range(PANEL):
                c = jnp.broadcast_to(ra[k][:, nxt + i : nxt + i + 1], (1, n))
                na = na - c * ra[k]
                ne = ne - c * re[k]
            d[row, 0:n] = na
            d[row, n : 2 * n] = ne
        far = nxt + PANEL
        if far < n:
            y = d[b : b + PANEL, :]
            d[far:n, :] = d[far:n, :] - dot_tn(y[:, far:n], y)


def split(x):
    hi = x.astype(jnp.bfloat16)
    return hi, (x - hi.astype(jnp.float32)).astype(jnp.bfloat16)


def dot3(a, b):
    ah, al = a
    bh, bl = b

    def one(p, q):
        return jnp.dot(p, q, preferred_element_type=jnp.float32)

    return one(ah, bh) + (one(ah, bl) + one(al, bh))


def rows_of(pair, start, stop):
    return tuple(p[start:stop, :] for p in pair)


def columns_of(pair, start, stop):
    return tuple(p[:, start:stop] for p in pair)


def upper_pairs(n):
    return [(i, j) for i in range(n) for j in range(i, n)]


def masked(ref, count):
    rows = lax.broadcasted_iota(jnp.int32, ref.shape, 0)
    return jnp.where(rows < count, ref[...], 0.0)


def put_by_core(core, keep_ref, send_ref, half, place, tile):
    @pl.when(core == half)
    def _():
        keep_ref[place] = tile

    @pl.when(core != half)
    def _():
        send_ref[place] = tile


def products_kernel(scalars, basis_ref, block_ref, keep_ref, send_ref, *, weight):
    count, core = scalars[0], scalars[1]
    basis = masked(basis_ref, count)
    block = masked(block_ref, count)
    turned = split(jnp.transpose(basis * weight))
    basis = split(basis)
    block = split(block)
    m, k = basis_ref.shape[1] // BLOCK, block_ref.shape[1] // BLOCK
    half_size = keep_ref.shape[0]
    position = 0
    for i in range(m):
        left = rows_of(turned, i * BLOCK, (i + 1) * BLOCK)
        own = dot3(left, columns_of(basis, i * BLOCK, m * BLOCK))
        cross = dot3(left, block)
        tiles = [own[:, j * BLOCK : (j + 1) * BLOCK] for j in range(m - i)]
        tiles += [cross[:, j * BLOCK : (j + 1) * BLOCK] for j in range(k)]
        for tile in tiles:
            put_by_core(
                core, keep_ref, send_ref, position // half_size, position % half_size, tile
            )
            position += 1


def residual_kernel(
    scalars, own_ref, other_ref, basis_ref, block_ref, residual_ref, keep_ref, send_ref,
    s_hi, s_lo, *, weight
):
    count, core = scalars[0], scalars[1]
    m, k = basis_ref.shape[1] // BLOCK, block_ref.shape[1] // BLOCK
    half_size = own_ref.shape[0]
    first = core == 0

    def tile_at(position):
        mine, theirs = own_ref[position % half_size], other_ref[position % half_size]
        swap = first if position < half_size else jnp.logical_not(first)
        return jnp.where(swap, mine, theirs)

    position = 0
    coeffs = []
    eye = identity(BLOCK)
    for i in range(m):
        for j in range(i, m):
            tile = -tile_at(position)
            position += 1
            if i == j:
                tile = eye + tile
            hi, lo = split(tile)
            s_hi[i * BLOCK : (i + 1) * BLOCK, j * BLOCK : (j + 1) * BLOCK] = hi
            s_lo[i * BLOCK : (i + 1) * BLOCK, j * BLOCK : (j + 1) * BLOCK] = lo
            if i != j:
                hi, lo = split(jnp.transpose(tile))
                s_hi[j * BLOCK : (j + 1) * BLOCK, i * BLOCK : (i + 1) * BLOCK] = hi
                s_lo[j * BLOCK : (j + 1) * BLOCK, i * BLOCK : (i + 1) * BLOCK] = lo
        row = []
        for j in range(k):
            row.append(tile_at(position))
            position += 1
        coeffs.append(jnp.concatenate(row, axis=1))
    coeffs = jnp.concatenate(coeffs, axis=0)
    total = coeffs + dot3((s_hi[...], s_lo[...]), split(coeffs))
    basis = split(masked(basis_ref, count))
    residual = masked(block_ref, count) - dot3(basis, split(total))
    residual_ref[...] = residual
    turned = split(jnp.transpose(residual * weight))
    residual = split(residual)
    half_size = keep_ref.shape[0]
    position = 0
    for i in range(k):
        row = dot3(
            rows_of(turned, i * BLOCK, (i + 1) * BLOCK), columns_of(residual, i * BLOCK, k * BLOCK)
        )
        for j in range(k - i):
            put_by_core(
                core, keep_ref, send_ref, position // half_size, position % half_size,
                row[:, j * BLOCK : (j + 1) * BLOCK],
            )
            position += 1


def factor_kernel(scalars, own_ref, other_ref, residual_ref, new_ref, factor_ref, w, d):
    size = residual_ref.shape[1]
    first = scalars[1] == 0
    half_size = own_ref.shape[0]
    w[:, size : 2 * size] = identity(size)
    for position, (i, j) in enumerate(upper_pairs(size // BLOCK)):
        swap = first if position < half_size else jnp.logical_not(first)
        w[i * BLOCK : (i + 1) * BLOCK, j * BLOCK : (j + 1) * BLOCK] = jnp.where(
            swap, own_ref[position % half_size], other_ref[position % half_size]
        )

    def outer(k, carry):
        o = pl.multiple_of(k * BLOCK, BLOCK)
        d[:, 0:BLOCK] = w[pl.ds(o, BLOCK), pl.ds(o, BLOCK)]
        d[:, BLOCK : 2 * BLOCK] = identity(BLOCK)
        eliminate_block(d)
        w[pl.ds(o, BLOCK), :] = dot_nn(d[:, BLOCK : 2 * BLOCK], w[pl.ds(o, BLOCK), :])
        w[pl.ds(o, BLOCK), pl.ds(o, BLOCK)] = d[:, 0:BLOCK]

        def inner(i, c):
            q = pl.multiple_of(i * BLOCK, BLOCK)
            w[pl.ds(q, BLOCK), :] = w[pl.ds(q, BLOCK), :] - dot_tn(
                w[pl.ds(o, BLOCK), pl.ds(q, BLOCK)], w[pl.ds(o, BLOCK), :]
            )
            return c

        return lax.fori_loop(k + 1, size // BLOCK, inner, carry)

    lax.fori_loop(0, size // BLOCK, outer, 0)
    upper = lax.broadcasted_iota(jnp.int32, (size, size), 0) <= lax.broadcasted_iota(
        jnp.int32, (size, size), 1
    )
    factor_ref[...] = jnp.where(upper, w[:, 0:size], 0.0)
    new_ref[...] = dot_nt(residual_ref[...], w[:, size : 2 * size])


def call(kernel, out_shapes, scratch, name):
    def run(scalars, *arrays):
        vmem = pl.BlockSpec(memory_space=pltpu.VMEM)
        return pl.pallas_call(
            kernel,
            out_shape=[jax.ShapeDtypeStruct(s, jnp.float32) for s in out_shapes],
            in_specs=[pl.BlockSpec(memory_space=pltpu.SMEM)] + [vmem] * len(arrays),
            out_specs=[vmem] * len(out_shapes),
            scratch_shapes=scratch,
            compiler_params=pltpu.CompilerParams(vmem_limit_bytes=48 << 20),
            name=name,
        )(scalars, *arrays)

    return run


def swap_cores(x):
    return lax.ppermute(x, "row_2", [(0, 1), (1, 0)])


def exchange(x, axes):
    return lax.all_to_all(x, axes, 0, 0, tiled=True)


def to_all(x, axes):
    count = lax.axis_size(axes)
    return exchange(jnp.broadcast_to(x[None], (count, *x.shape)), axes)


def sum_halves(keep, send, spread):
    total = (keep + swap_cores(send)).reshape(-1, 8, 128)
    plane = lax.axis_size(PLANE)
    part = jnp.sum(exchange(total.reshape(plane, -1, 8, 128), PLANE), axis=0)
    if spread:
        grp = lax.axis_size("grp")
        lines = part.shape[0]
        padded = jnp.pad(part, ((0, -lines % grp), (0, 0), (0, 0)))
        part = jnp.sum(exchange(padded.reshape(grp, -1, 8, 128), "grp"), axis=0)
        part = to_all(part, "grp").reshape(-1, 8, 128)[:lines]
    else:
        part = jnp.sum(to_all(part, "grp"), axis=0)
    whole = to_all(part, PLANE).reshape(keep.shape)
    return whole, swap_cores(whole)


def body(basis, block, counts):
    row_slots, size = block.shape
    m, k = basis.shape[1] // BLOCK, size // BLOCK
    devices = lax.axis_size("grp") * lax.axis_size(ROW)
    weight = 1.0 / (row_slots * devices)
    scalars = jnp.stack([counts[0, 0], lax.axis_index("row_2").astype(jnp.int32)])
    tiles = (m * (m + 1) // 2 + m * k) // 2
    gram_tiles = k * (k + 1) // 4
    half = (tiles, BLOCK, BLOCK)
    gram_half = (gram_tiles, BLOCK, BLOCK)
    keep, send = call(
        functools.partial(products_kernel, weight=weight), [half, half], [], "products"
    )(scalars, basis, block)
    own, other = sum_halves(keep, send, True)
    wide = pltpu.VMEM((m * BLOCK, m * BLOCK), jnp.bfloat16)
    residual, keep, send = call(
        functools.partial(residual_kernel, weight=weight),
        [block.shape, gram_half, gram_half],
        [wide, wide],
        "residual",
    )(scalars, own, other, basis, block)
    own, other = sum_halves(keep, send, False)
    new_block, factor = call(
        factor_kernel,
        [block.shape, (size, size)],
        [
            pltpu.VMEM((size, 2 * size), jnp.float32),
            pltpu.VMEM((BLOCK, 2 * BLOCK), jnp.float32),
        ],
        "factor",
    )(scalars, own, other, residual)
    return new_block, factor


def solution(mesh):
    torus = Mesh(
        mesh.devices.reshape(mesh.shape["grp"], 4, 4, 2), ("grp", "row_0", "row_1", "row_2")
    )
    in_specs = (P(GRP_ROW, None), P(GRP_ROW, None), P("grp", ROW))
    out_specs = (P(GRP_ROW, None), P())
    return jax.shard_map(body, mesh=torus, in_specs=in_specs, out_specs=out_specs, check_vma=False)
```

```python
import functools

import jax
import jax.numpy as jnp
from jax import lax
from jax.experimental import pallas as pl
from jax.experimental.pallas import tpu as pltpu
from jax.sharding import Mesh
from jax.sharding import PartitionSpec as P

ROW = ("row_0", "row_1", "row_2")
GRP_ROW = ("grp", "row_0", "row_1", "row_2")
PLANE = ("row_0", "row_1")

BLOCK = 128
STEP = 64
PANEL = 8
HIGHEST = lax.Precision.HIGHEST


def identity(n):
    return (
        lax.broadcasted_iota(jnp.int32, (n, n), 0) == lax.broadcasted_iota(jnp.int32, (n, n), 1)
    ).astype(jnp.float32)


def spread(x):
    return jnp.broadcast_to(x, (PANEL, BLOCK))


def tree_sum(terms):
    while len(terms) > 1:
        terms = [a + b for a, b in zip(terms[::2], terms[1::2])]
    return terms[0]


def eliminate(v, a0):
    n = len(v)
    row = lax.broadcasted_iota(jnp.int32, (PANEL, BLOCK), 0)
    panel = range(PANEL)
    diag = [spread(v[0][:, a0 + j : a0 + j + 1]) for j in panel]
    for p in range(n):
        base = a0 + PANEL * p
        turned = {
            q: [spread(v[q][:, base + j : base + j + 1]) for j in panel] for q in range(p + 1, n)
        }
        if p + 1 < n:
            after = base + PANEL
            ahead = [spread(v[p + 1][:, after + j : after + j + 1]) for j in panel]
        current = v[p]
        rows, coefs, inverses = [], [], []
        scale = None
        for k in panel:
            inv = lax.rsqrt(spread(diag[k][k : k + 1, :]))
            col = diag[k] * inv
            r = [spread(col[j : j + 1, :]) if j > k else None for j in panel]
            for j in range(k + 1, PANEL):
                diag[j] = diag[j] - col * r[j]
            own = spread(current[k : k + 1, :]) * inv
            rows.append(own)
            if k < PANEL - 1:
                current = current - jnp.where(row > k, col, 0.0) * own
            scale = inv if scale is None else jnp.where(row >= k, inv, scale)
            coefs.append(r)
            inverses.append(inv)
        v[p] = current * scale
        for q in range(p + 1, n):
            t = turned[q]
            for k in panel:
                t[k] = t[k] * inverses[k]
                for j in range(k + 1, PANEL):
                    t[j] = t[j] - t[k] * coefs[k][j]
            v[q] = v[q] - tree_sum([t[k] * rows[k] for k in panel])
            if q == p + 1:
                diag = [
                    ahead[j] - tree_sum([t[k] * spread(t[k][j : j + 1, :]) for k in panel])
                    for j in panel
                ]
    return v


def twice_left(x):
    hi, lo = split(x)
    lane = lax.broadcasted_iota(jnp.int32, x.shape, 1)
    both = jnp.where(lane < STEP, hi.astype(jnp.float32), lo.astype(jnp.float32))
    both = both.astype(jnp.bfloat16)
    return jnp.concatenate([both, both], axis=1)


def stacked_dot(left4, x):
    hi, lo = split(x)
    return jnp.dot(
        left4, jnp.concatenate([hi, hi, lo, lo], axis=0), preferred_element_type=jnp.float32
    )


def stacked_dot_tn(a, b):
    ah, al = split(a)
    bh, bl = split(b)
    return lax.dot_general(
        jnp.concatenate([ah, al, ah, al], axis=0),
        jnp.concatenate([bh, bh, bl, bl], axis=0),
        (((0,), (0,)), ((), ())),
        preferred_element_type=jnp.float32,
    )


def split(x):
    hi = x.astype(jnp.bfloat16)
    return hi, (x - hi.astype(jnp.float32)).astype(jnp.bfloat16)


def dot3(a, b):
    ah, al = a
    bh, bl = b

    def one(p, q):
        return jnp.dot(p, q, preferred_element_type=jnp.float32)

    return one(ah, bh) + (one(ah, bl) + one(al, bh))


def rows_of(pair, start, stop):
    return tuple(p[start:stop, :] for p in pair)


def columns_of(pair, start, stop):
    return tuple(p[:, start:stop] for p in pair)


def upper_pairs(n):
    return [(i, j) for i in range(n) for j in range(i, n)]


def masked(ref, count):
    rows = lax.broadcasted_iota(jnp.int32, ref.shape, 0)
    return jnp.where(rows < count, ref[...], 0.0)


def put_by_core(core, keep_ref, send_ref, half, place, tile):
    @pl.when(core == half)
    def _():
        keep_ref[place] = tile

    @pl.when(core != half)
    def _():
        send_ref[place] = tile


def products_kernel(scalars, basis_ref, block_ref, keep_ref, send_ref, *, weight):
    count, core = scalars[0], scalars[1]
    basis = masked(basis_ref, count)
    block = masked(block_ref, count)
    turned = split(jnp.transpose(basis * weight))
    basis = split(basis)
    block = split(block)
    m, k = basis_ref.shape[1] // BLOCK, block_ref.shape[1] // BLOCK
    half_size = keep_ref.shape[0]
    position = 0
    for i in range(m):
        left = rows_of(turned, i * BLOCK, (i + 1) * BLOCK)
        own = dot3(left, columns_of(basis, i * BLOCK, m * BLOCK))
        cross = dot3(left, block)
        rest = jnp.dot(
            left[1],
            basis[1][:, i * BLOCK : (i + 1) * BLOCK],
            preferred_element_type=jnp.float32,
        )
        tiles = [own[:, j * BLOCK : (j + 1) * BLOCK] for j in range(m - i)]
        tiles[0] = tiles[0] + rest
        tiles += [cross[:, j * BLOCK : (j + 1) * BLOCK] for j in range(k)]
        for tile in tiles:
            put_by_core(
                core, keep_ref, send_ref, position // half_size, position % half_size, tile
            )
            position += 1


def residual_kernel(
    scalars, own_ref, other_ref, basis_ref, block_ref, residual_ref, keep_ref, send_ref,
    s_hi, s_lo, *, weight
):
    count, core = scalars[0], scalars[1]
    m, k = basis_ref.shape[1] // BLOCK, block_ref.shape[1] // BLOCK
    half_size = own_ref.shape[0]
    first = core == 0

    def tile_at(position):
        mine, theirs = own_ref[position % half_size], other_ref[position % half_size]
        swap = first if position < half_size else jnp.logical_not(first)
        return jnp.where(swap, mine, theirs)

    position = 0
    coeffs = []
    eye = identity(BLOCK)
    for i in range(m):
        for j in range(i, m):
            tile = -tile_at(position)
            position += 1
            if i == j:
                tile = eye + tile
            hi, lo = split(tile)
            s_hi[i * BLOCK : (i + 1) * BLOCK, j * BLOCK : (j + 1) * BLOCK] = hi
            s_lo[i * BLOCK : (i + 1) * BLOCK, j * BLOCK : (j + 1) * BLOCK] = lo
            if i != j:
                hi, lo = split(jnp.transpose(tile))
                s_hi[j * BLOCK : (j + 1) * BLOCK, i * BLOCK : (i + 1) * BLOCK] = hi
                s_lo[j * BLOCK : (j + 1) * BLOCK, i * BLOCK : (i + 1) * BLOCK] = lo
        row = []
        for j in range(k):
            row.append(tile_at(position))
            position += 1
        coeffs.append(jnp.concatenate(row, axis=1))
    coeffs = jnp.concatenate(coeffs, axis=0)
    total = coeffs + dot3((s_hi[...], s_lo[...]), split(coeffs))
    basis = masked(basis_ref, count)
    residual = masked(block_ref, count) - jnp.dot(
        basis, total, precision=HIGHEST, preferred_element_type=jnp.float32
    )
    residual_ref[...] = residual
    turned = split(jnp.transpose(residual * weight))
    residual = split(residual)
    half_size = keep_ref.shape[0]
    position = 0
    for i in range(k):
        row = dot3(
            rows_of(turned, i * BLOCK, (i + 1) * BLOCK), columns_of(residual, i * BLOCK, k * BLOCK)
        )
        for j in range(k - i):
            put_by_core(
                core, keep_ref, send_ref, position // half_size, position % half_size,
                row[:, j * BLOCK : (j + 1) * BLOCK],
            )
            position += 1


def dot3_nt(a, b):
    ah, al = a
    bh, bl = b

    def one(p, q):
        return lax.dot_general(p, q, (((1,), (1,)), ((), ())), preferred_element_type=jnp.float32)

    return one(ah, bh) + (one(ah, bl) + one(al, bh))


def factor_kernel(scalars, own_ref, other_ref, residual_ref, new_ref, factor_ref, w, inv_ref):
    size = residual_ref.shape[1]
    first = scalars[1] == 0
    half_size = own_ref.shape[0]
    zero = jnp.zeros((BLOCK, BLOCK), jnp.float32)
    for position, (i, j) in enumerate(upper_pairs(size // BLOCK)):
        swap = first if position < half_size else jnp.logical_not(first)
        w[i * BLOCK : (i + 1) * BLOCK, j * BLOCK : (j + 1) * BLOCK] = jnp.where(
            swap, own_ref[position % half_size], other_ref[position % half_size]
        )
        if i != j:
            w[j * BLOCK : (j + 1) * BLOCK, i * BLOCK : (i + 1) * BLOCK] = zero
    residual = split(residual_ref[...])
    zero = jnp.zeros((STEP, BLOCK), jnp.float32)
    lane = lax.broadcasted_iota(jnp.int32, (PANEL, BLOCK), 1)
    row = lax.broadcasted_iota(jnp.int32, (PANEL, BLOCK), 0)
    lanes = lax.broadcasted_iota(jnp.int32, (STEP, BLOCK), 1)
    rows = lax.broadcasted_iota(jnp.int32, (STEP, BLOCK), 0)
    following = None
    for k in range(size // STEP):
        o = k * STEP
        end = o + STEP
        lo = o // BLOCK * BLOCK
        hi = lo + BLOCK
        a0 = o - lo
        e0 = STEP - a0
        square = w[o:end, lo:hi] if following is None else following
        v = []
        for q in range(STEP // PANEL):
            eye = (lane - e0 == row + PANEL * q).astype(jnp.float32)
            inside = (lane >= a0) & (lane < a0 + STEP)
            v.append(jnp.where(inside, square[PANEL * q : PANEL * q + PANEL, :], eye))
        d = jnp.concatenate(eliminate(v, a0), axis=0)
        swapped = pltpu.roll(d, STEP, 1)
        here = (lanes >= a0) & (lanes < a0 + STEP)
        left4 = twice_left(jnp.where(here, swapped, d))
        if end < size:
            lo2 = end // BLOCK * BLOCK
            part = stacked_dot(left4, w[o:end, lo2 : lo2 + BLOCK])
            drop = stacked_dot_tn(part, part)[end - lo2 : end - lo2 + STEP, :]
            following = w[end : end + STEP, lo2 : lo2 + BLOCK] - drop
        z = stacked_dot(left4, w[o:end, :])
        z_here = z[:, lo:hi]
        upper = jnp.where(
            here & (lanes - a0 >= rows), d, jnp.where(lanes >= a0 + STEP, z_here, 0.0)
        )
        lower = jnp.where(
            here, jnp.where(lanes - a0 <= rows, swapped, 0.0), jnp.where(lanes < a0, z_here, 0.0)
        )
        for c in range(0, size, BLOCK):
            band = slice(c, c + BLOCK)
            factor_ref[o:end, band] = zero if c < lo else (upper if c == lo else z[:, band])
            inv_ref[o:end, band] = z[:, band] if c < lo else (lower if c == lo else zero)
        if end < size:
            pieces = [z[:, :lo]] if lo else []
            pieces.append(jnp.where(here, swapped, z_here))
            if hi < size:
                pieces.append(z[:, hi:])
            first_lane = end // BLOCK * BLOCK
            drop = stacked_dot_tn(z[:, first_lane:], jnp.concatenate(pieces, axis=1))
            column = lax.broadcasted_iota(jnp.int32, (size - end, size), 1)
            w[end:size, :] = (
                jnp.where((column >= o) & (column < end), 0.0, w[end:size, :])
                - drop[end - first_lane :, :]
            )
        if end == hi:
            new_ref[:, lo:hi] = dot3_nt(
                columns_of(residual, 0, hi), split(inv_ref[lo:hi, 0:hi])
            )


def call(kernel, out_shapes, scratch, name):
    def run(scalars, *arrays):
        vmem = pl.BlockSpec(memory_space=pltpu.VMEM)
        return pl.pallas_call(
            kernel,
            out_shape=[jax.ShapeDtypeStruct(s, jnp.float32) for s in out_shapes],
            in_specs=[pl.BlockSpec(memory_space=pltpu.SMEM)] + [vmem] * len(arrays),
            out_specs=[vmem] * len(out_shapes),
            scratch_shapes=scratch,
            compiler_params=pltpu.CompilerParams(vmem_limit_bytes=48 << 20),
            name=name,
        )(scalars, *arrays)

    return run


def swap_cores(x):
    return lax.ppermute(x, "row_2", [(0, 1), (1, 0)])


def exchange(x, axes):
    return lax.all_to_all(x, axes, 0, 0, tiled=True)


def to_all(x, axes):
    count = lax.axis_size(axes)
    return exchange(jnp.broadcast_to(x[None], (count, *x.shape)), axes)


def sum_halves(keep, send, spread):
    total = (keep + swap_cores(send)).reshape(-1, 8, 128)
    plane = lax.axis_size(PLANE)
    part = jnp.sum(exchange(total.reshape(plane, -1, 8, 128), PLANE), axis=0)
    if spread:
        grp = lax.axis_size("grp")
        lines = part.shape[0]
        padded = jnp.pad(part, ((0, -lines % grp), (0, 0), (0, 0)))
        part = jnp.sum(exchange(padded.reshape(grp, -1, 8, 128), "grp"), axis=0)
        part = to_all(part, "grp").reshape(-1, 8, 128)[:lines]
    else:
        part = jnp.sum(to_all(part, "grp"), axis=0)
    whole = to_all(part, PLANE).reshape(keep.shape)
    return whole, swap_cores(whole)


def body(basis, block, counts):
    row_slots, size = block.shape
    m, k = basis.shape[1] // BLOCK, size // BLOCK
    devices = lax.axis_size("grp") * lax.axis_size(ROW)
    weight = 1.0 / (row_slots * devices)
    scalars = jnp.stack([counts[0, 0], lax.axis_index("row_2").astype(jnp.int32)])
    tiles = (m * (m + 1) // 2 + m * k) // 2
    gram_tiles = k * (k + 1) // 4
    half = (tiles, BLOCK, BLOCK)
    gram_half = (gram_tiles, BLOCK, BLOCK)
    keep, send = call(
        functools.partial(products_kernel, weight=weight), [half, half], [], "products"
    )(scalars, basis, block)
    own, other = sum_halves(keep, send, True)
    wide = pltpu.VMEM((m * BLOCK, m * BLOCK), jnp.bfloat16)
    residual, keep, send = call(
        functools.partial(residual_kernel, weight=weight),
        [block.shape, gram_half, gram_half],
        [wide, wide],
        "residual",
    )(scalars, own, other, basis, block)
    own, other = sum_halves(keep, send, False)
    new_block, factor = call(
        factor_kernel,
        [block.shape, (size, size)],
        [
            pltpu.VMEM((size, size), jnp.float32),
            pltpu.VMEM((size, size), jnp.float32),
        ],
        "factor",
    )(scalars, own, other, residual)
    return new_block, factor


def solution(mesh):
    torus = Mesh(
        mesh.devices.reshape(mesh.shape["grp"], 4, 4, 2), ("grp", "row_0", "row_1", "row_2")
    )
    in_specs = (P(GRP_ROW, None), P(GRP_ROW, None), P("grp", ROW))
    out_specs = (P(GRP_ROW, None), P())
    return jax.shard_map(body, mesh=torus, in_specs=in_specs, out_specs=out_specs, check_vma=False)
```

```python
import functools

import jax
import jax.numpy as jnp
from jax import lax
from jax.experimental import pallas as pl
from jax.experimental.pallas import tpu as pltpu
from jax.sharding import Mesh
from jax.sharding import PartitionSpec as P

ROW = ("row_0", "row_1", "row_2")
GRP = ("grp_0", "grp_1")
GRP_ROW = (*GRP, *ROW)
PLANE = ("row_0", "row_1")
SLAB = ("grp_1", "row_0", "row_1")

BLOCK = 128
STEP = 64
PANEL = 8
HIGHEST = lax.Precision.HIGHEST


def identity(n):
    return (
        lax.broadcasted_iota(jnp.int32, (n, n), 0) == lax.broadcasted_iota(jnp.int32, (n, n), 1)
    ).astype(jnp.float32)


def spread(x):
    return jnp.broadcast_to(x, (PANEL, BLOCK))


def tree_sum(terms):
    while len(terms) > 1:
        terms = [a + b for a, b in zip(terms[::2], terms[1::2])]
    return terms[0]


def eliminate(v, a0):
    n = len(v)
    row = lax.broadcasted_iota(jnp.int32, (PANEL, BLOCK), 0)
    panel = range(PANEL)
    diag = [spread(v[0][:, a0 + j : a0 + j + 1]) for j in panel]
    for p in range(n):
        base = a0 + PANEL * p
        turned = {
            q: [spread(v[q][:, base + j : base + j + 1]) for j in panel] for q in range(p + 1, n)
        }
        if p + 1 < n:
            after = base + PANEL
            ahead = [spread(v[p + 1][:, after + j : after + j + 1]) for j in panel]
        current = v[p]
        rows, coefs, inverses = [], [], []
        scale = None
        for k in panel:
            inv = lax.rsqrt(spread(diag[k][k : k + 1, :]))
            col = diag[k] * inv
            r = [spread(col[j : j + 1, :]) if j > k else None for j in panel]
            for j in range(k + 1, PANEL):
                diag[j] = diag[j] - col * r[j]
            own = spread(current[k : k + 1, :]) * inv
            rows.append(own)
            if k < PANEL - 1:
                current = current - jnp.where(row > k, col, 0.0) * own
            scale = inv if scale is None else jnp.where(row >= k, inv, scale)
            coefs.append(r)
            inverses.append(inv)
        v[p] = current * scale
        for q in range(p + 1, n):
            t = turned[q]
            for k in panel:
                t[k] = t[k] * inverses[k]
                for j in range(k + 1, PANEL):
                    t[j] = t[j] - t[k] * coefs[k][j]
            v[q] = v[q] - tree_sum([t[k] * rows[k] for k in panel])
            if q == p + 1:
                diag = [
                    ahead[j] - tree_sum([t[k] * spread(t[k][j : j + 1, :]) for k in panel])
                    for j in panel
                ]
    return v


def twice_left(x):
    hi, lo = split(x)
    lane = lax.broadcasted_iota(jnp.int32, x.shape, 1)
    both = jnp.where(lane < STEP, hi.astype(jnp.float32), lo.astype(jnp.float32))
    both = both.astype(jnp.bfloat16)
    return jnp.concatenate([both, both], axis=1)


def stacked_dot(left4, x):
    hi, lo = split(x)
    return jnp.dot(
        left4, jnp.concatenate([hi, hi, lo, lo], axis=0), preferred_element_type=jnp.float32
    )


def stacked_dot_tn(a, b):
    ah, al = split(a)
    bh, bl = split(b)
    return lax.dot_general(
        jnp.concatenate([ah, al, ah, al], axis=0),
        jnp.concatenate([bh, bh, bl, bl], axis=0),
        (((0,), (0,)), ((), ())),
        preferred_element_type=jnp.float32,
    )


def split(x):
    hi = x.astype(jnp.bfloat16)
    return hi, (x - hi.astype(jnp.float32)).astype(jnp.bfloat16)


def dot3(a, b):
    ah, al = a
    bh, bl = b

    def one(p, q):
        return jnp.dot(p, q, preferred_element_type=jnp.float32)

    return one(ah, bh) + (one(ah, bl) + one(al, bh))


def rows_of(pair, start, stop):
    return tuple(p[start:stop, :] for p in pair)


def columns_of(pair, start, stop):
    return tuple(p[:, start:stop] for p in pair)


def upper_pairs(n):
    return [(i, j) for i in range(n) for j in range(i, n)]


def masked(ref, count):
    rows = lax.broadcasted_iota(jnp.int32, ref.shape, 0)
    return jnp.where(rows < count, ref[...], 0.0)


def put_by_core(core, keep_ref, send_ref, half, place, tile):
    @pl.when(core == half)
    def _():
        keep_ref[place] = tile

    @pl.when(core != half)
    def _():
        send_ref[place] = tile


def products_kernel(scalars, basis_ref, block_ref, keep_ref, send_ref, *, weight):
    count, core = scalars[0], scalars[1]
    basis = masked(basis_ref, count)
    block = masked(block_ref, count)
    turned = split(jnp.transpose(basis * weight))
    basis = split(basis)
    block = split(block)
    m, k = basis_ref.shape[1] // BLOCK, block_ref.shape[1] // BLOCK
    half_size = keep_ref.shape[0]
    position = 0
    for i in range(m):
        left = rows_of(turned, i * BLOCK, (i + 1) * BLOCK)
        own = dot3(left, columns_of(basis, i * BLOCK, m * BLOCK))
        cross = dot3(left, block)
        rest = jnp.dot(
            left[1],
            basis[1][:, i * BLOCK : (i + 1) * BLOCK],
            preferred_element_type=jnp.float32,
        )
        tiles = [own[:, j * BLOCK : (j + 1) * BLOCK] for j in range(m - i)]
        tiles[0] = tiles[0] + rest
        tiles += [cross[:, j * BLOCK : (j + 1) * BLOCK] for j in range(k)]
        for tile in tiles:
            put_by_core(
                core, keep_ref, send_ref, position // half_size, position % half_size, tile
            )
            position += 1


def residual_kernel(
    scalars, own_ref, other_ref, basis_ref, block_ref, residual_ref, keep_ref, send_ref,
    s_hi, s_lo, *, weight
):
    count, core = scalars[0], scalars[1]
    m, k = basis_ref.shape[1] // BLOCK, block_ref.shape[1] // BLOCK
    half_size = own_ref.shape[0]
    first = core == 0

    def tile_at(position):
        mine, theirs = own_ref[position % half_size], other_ref[position % half_size]
        swap = first if position < half_size else jnp.logical_not(first)
        return jnp.where(swap, mine, theirs)

    position = 0
    coeffs = []
    eye = identity(BLOCK)
    for i in range(m):
        for j in range(i, m):
            tile = -tile_at(position)
            position += 1
            if i == j:
                tile = eye + tile
            hi, lo = split(tile)
            s_hi[i * BLOCK : (i + 1) * BLOCK, j * BLOCK : (j + 1) * BLOCK] = hi
            s_lo[i * BLOCK : (i + 1) * BLOCK, j * BLOCK : (j + 1) * BLOCK] = lo
            if i != j:
                hi, lo = split(jnp.transpose(tile))
                s_hi[j * BLOCK : (j + 1) * BLOCK, i * BLOCK : (i + 1) * BLOCK] = hi
                s_lo[j * BLOCK : (j + 1) * BLOCK, i * BLOCK : (i + 1) * BLOCK] = lo
        row = []
        for j in range(k):
            row.append(tile_at(position))
            position += 1
        coeffs.append(jnp.concatenate(row, axis=1))
    coeffs = jnp.concatenate(coeffs, axis=0)
    total = coeffs + dot3((s_hi[...], s_lo[...]), split(coeffs))
    basis = masked(basis_ref, count)
    residual = masked(block_ref, count) - jnp.dot(
        basis, total, precision=HIGHEST, preferred_element_type=jnp.float32
    )
    residual_ref[...] = residual
    turned = split(jnp.transpose(residual * weight))
    residual = split(residual)
    half_size = keep_ref.shape[0]
    position = 0
    for i in range(k):
        row = dot3(
            rows_of(turned, i * BLOCK, (i + 1) * BLOCK), columns_of(residual, i * BLOCK, k * BLOCK)
        )
        for j in range(k - i):
            put_by_core(
                core, keep_ref, send_ref, position // half_size, position % half_size,
                row[:, j * BLOCK : (j + 1) * BLOCK],
            )
            position += 1


def dot3_nt(a, b):
    ah, al = a
    bh, bl = b

    def one(p, q):
        return lax.dot_general(p, q, (((1,), (1,)), ((), ())), preferred_element_type=jnp.float32)

    return one(ah, bh) + (one(ah, bl) + one(al, bh))


def factor_kernel(scalars, own_ref, other_ref, residual_ref, new_ref, factor_ref, w, inv_ref):
    size = residual_ref.shape[1]
    first = scalars[1] == 0
    half_size = own_ref.shape[0]
    zero = jnp.zeros((BLOCK, BLOCK), jnp.float32)
    for position, (i, j) in enumerate(upper_pairs(size // BLOCK)):
        swap = first if position < half_size else jnp.logical_not(first)
        w[i * BLOCK : (i + 1) * BLOCK, j * BLOCK : (j + 1) * BLOCK] = jnp.where(
            swap, own_ref[position % half_size], other_ref[position % half_size]
        )
        if i != j:
            w[j * BLOCK : (j + 1) * BLOCK, i * BLOCK : (i + 1) * BLOCK] = zero
    residual = split(residual_ref[...])
    zero = jnp.zeros((STEP, BLOCK), jnp.float32)
    lane = lax.broadcasted_iota(jnp.int32, (PANEL, BLOCK), 1)
    row = lax.broadcasted_iota(jnp.int32, (PANEL, BLOCK), 0)
    lanes = lax.broadcasted_iota(jnp.int32, (STEP, BLOCK), 1)
    rows = lax.broadcasted_iota(jnp.int32, (STEP, BLOCK), 0)
    following = None
    for k in range(size // STEP):
        o = k * STEP
        end = o + STEP
        lo = o // BLOCK * BLOCK
        hi = lo + BLOCK
        a0 = o - lo
        e0 = STEP - a0
        square = w[o:end, lo:hi] if following is None else following
        v = []
        for q in range(STEP // PANEL):
            eye = (lane - e0 == row + PANEL * q).astype(jnp.float32)
            inside = (lane >= a0) & (lane < a0 + STEP)
            v.append(jnp.where(inside, square[PANEL * q : PANEL * q + PANEL, :], eye))
        d = jnp.concatenate(eliminate(v, a0), axis=0)
        swapped = pltpu.roll(d, STEP, 1)
        here = (lanes >= a0) & (lanes < a0 + STEP)
        left4 = twice_left(jnp.where(here, swapped, d))
        if end < size:
            lo2 = end // BLOCK * BLOCK
            part = stacked_dot(left4, w[o:end, lo2 : lo2 + BLOCK])
            drop = stacked_dot_tn(part, part)[end - lo2 : end - lo2 + STEP, :]
            following = w[end : end + STEP, lo2 : lo2 + BLOCK] - drop
        z = stacked_dot(left4, w[o:end, :])
        z_here = z[:, lo:hi]
        upper = jnp.where(
            here & (lanes - a0 >= rows), d, jnp.where(lanes >= a0 + STEP, z_here, 0.0)
        )
        lower = jnp.where(
            here, jnp.where(lanes - a0 <= rows, swapped, 0.0), jnp.where(lanes < a0, z_here, 0.0)
        )
        for c in range(0, size, BLOCK):
            band = slice(c, c + BLOCK)
            factor_ref[o:end, band] = zero if c < lo else (upper if c == lo else z[:, band])
            inv_ref[o:end, band] = z[:, band] if c < lo else (lower if c == lo else zero)
        if end < size:
            pieces = [z[:, :lo]] if lo else []
            pieces.append(jnp.where(here, swapped, z_here))
            if hi < size:
                pieces.append(z[:, hi:])
            first_lane = end // BLOCK * BLOCK
            drop = stacked_dot_tn(z[:, first_lane:], jnp.concatenate(pieces, axis=1))
            column = lax.broadcasted_iota(jnp.int32, (size - end, size), 1)
            w[end:size, :] = (
                jnp.where((column >= o) & (column < end), 0.0, w[end:size, :])
                - drop[end - first_lane :, :]
            )
        if end == hi:
            new_ref[:, lo:hi] = dot3_nt(
                columns_of(residual, 0, hi), split(inv_ref[lo:hi, 0:hi])
            )


def call(kernel, out_shapes, scratch, name):
    def run(scalars, *arrays):
        vmem = pl.BlockSpec(memory_space=pltpu.VMEM)
        return pl.pallas_call(
            kernel,
            out_shape=[jax.ShapeDtypeStruct(s, jnp.float32) for s in out_shapes],
            in_specs=[pl.BlockSpec(memory_space=pltpu.SMEM)] + [vmem] * len(arrays),
            out_specs=[vmem] * len(out_shapes),
            scratch_shapes=scratch,
            compiler_params=pltpu.CompilerParams(vmem_limit_bytes=48 << 20),
            name=name,
        )(scalars, *arrays)

    return run


def swap_cores(x):
    return lax.ppermute(x, "row_2", [(0, 1), (1, 0)])


def exchange(x, axes):
    return lax.all_to_all(x, axes, 0, 0, tiled=True)


def to_all(x, axes):
    count = lax.axis_size(axes)
    return exchange(jnp.broadcast_to(x[None], (count, *x.shape)), axes)


def sum_halves(keep, send, near, far):
    total = (keep + swap_cores(send)).reshape(lax.axis_size(near), -1, 8, 128)
    part = jnp.sum(exchange(total, near), axis=0)
    part = jnp.sum(to_all(part, far), axis=0)
    whole = to_all(part, near).reshape(keep.shape)
    return whole, swap_cores(whole)


def body(basis, block, counts):
    row_slots, size = block.shape
    m, k = basis.shape[1] // BLOCK, size // BLOCK
    devices = lax.axis_size(GRP) * lax.axis_size(ROW)
    weight = 1.0 / (row_slots * devices)
    scalars = jnp.stack([counts[0, 0], lax.axis_index("row_2").astype(jnp.int32)])
    tiles = (m * (m + 1) // 2 + m * k) // 2
    gram_tiles = k * (k + 1) // 4
    half = (tiles, BLOCK, BLOCK)
    gram_half = (gram_tiles, BLOCK, BLOCK)
    keep, send = call(
        functools.partial(products_kernel, weight=weight), [half, half], [], "products"
    )(scalars, basis, block)
    own, other = sum_halves(keep, send, SLAB, "grp_0")
    wide = pltpu.VMEM((m * BLOCK, m * BLOCK), jnp.bfloat16)
    residual, keep, send = call(
        functools.partial(residual_kernel, weight=weight),
        [block.shape, gram_half, gram_half],
        [wide, wide],
        "residual",
    )(scalars, own, other, basis, block)
    own, other = sum_halves(keep, send, PLANE, GRP)
    new_block, factor = call(
        factor_kernel,
        [block.shape, (size, size)],
        [
            pltpu.VMEM((size, size), jnp.float32),
            pltpu.VMEM((size, size), jnp.float32),
        ],
        "factor",
    )(scalars, own, other, residual)
    return new_block, factor


def solution(mesh):
    torus = Mesh(mesh.devices.reshape(mesh.shape["grp"] // 2, 2, 4, 4, 2), GRP_ROW)
    in_specs = (P(GRP_ROW, None), P(GRP_ROW, None), P(GRP, ROW))
    out_specs = (P(GRP_ROW, None), P())
    return jax.shard_map(body, mesh=torus, in_specs=in_specs, out_specs=out_specs, check_vma=False)
```

```python
import functools

import jax
import jax.numpy as jnp
from jax import lax
from jax.experimental import pallas as pl
from jax.experimental.pallas import tpu as pltpu
from jax.sharding import Mesh
from jax.sharding import PartitionSpec as P

ROW = ("row_0", "row_1", "row_2")
GRP = ("grp_0", "grp_1")
GRP_ROW = (*GRP, *ROW)
PLANE = ("row_0", "row_1")
SLAB = ("grp_1", "row_0", "row_1")

BLOCK = 128
STEP = 64
PANEL = 8
HIGHEST = lax.Precision.HIGHEST


def identity(n):
    return (
        lax.broadcasted_iota(jnp.int32, (n, n), 0) == lax.broadcasted_iota(jnp.int32, (n, n), 1)
    ).astype(jnp.float32)


def spread(x):
    return jnp.broadcast_to(x, (PANEL, BLOCK))


def tree_sum(terms):
    while len(terms) > 1:
        terms = [a + b for a, b in zip(terms[::2], terms[1::2])]
    return terms[0]


def eliminate(v, a0):
    n = len(v)
    row = lax.broadcasted_iota(jnp.int32, (PANEL, BLOCK), 0)
    panel = range(PANEL)
    diag = [spread(v[0][:, a0 + j : a0 + j + 1]) for j in panel]
    for p in range(n):
        base = a0 + PANEL * p
        turned = {
            q: [spread(v[q][:, base + j : base + j + 1]) for j in panel] for q in range(p + 1, n)
        }
        if p + 1 < n:
            after = base + PANEL
            ahead = [spread(v[p + 1][:, after + j : after + j + 1]) for j in panel]
        current = v[p]
        rows, coefs, inverses = [], [], []
        scale = None
        for k in panel:
            inv = lax.rsqrt(spread(diag[k][k : k + 1, :]))
            col = diag[k] * inv
            r = [spread(col[j : j + 1, :]) if j > k else None for j in panel]
            for j in range(k + 1, PANEL):
                diag[j] = diag[j] - col * r[j]
            own = spread(current[k : k + 1, :]) * inv
            rows.append(own)
            if k < PANEL - 1:
                current = current - jnp.where(row > k, col, 0.0) * own
            scale = inv if scale is None else jnp.where(row >= k, inv, scale)
            coefs.append(r)
            inverses.append(inv)
        v[p] = current * scale
        for q in range(p + 1, n):
            t = turned[q]
            for k in panel:
                t[k] = t[k] * inverses[k]
                for j in range(k + 1, PANEL):
                    t[j] = t[j] - t[k] * coefs[k][j]
            v[q] = v[q] - tree_sum([t[k] * rows[k] for k in panel])
            if q == p + 1:
                diag = [
                    ahead[j] - tree_sum([t[k] * spread(t[k][j : j + 1, :]) for k in panel])
                    for j in panel
                ]
    return v


def twice_left(x):
    hi, lo = split(x)
    lane = lax.broadcasted_iota(jnp.int32, x.shape, 1)
    both = jnp.where(lane < STEP, hi.astype(jnp.float32), lo.astype(jnp.float32))
    both = both.astype(jnp.bfloat16)
    return jnp.concatenate([both, both], axis=1)


def stacked_dot(left4, x):
    hi, lo = split(x)
    return jnp.dot(
        left4, jnp.concatenate([hi, hi, lo, lo], axis=0), preferred_element_type=jnp.float32
    )


def stacked_dot_tn(a, b):
    ah, al = split(a)
    bh, bl = split(b)
    return lax.dot_general(
        jnp.concatenate([ah, al, ah, al], axis=0),
        jnp.concatenate([bh, bh, bl, bl], axis=0),
        (((0,), (0,)), ((), ())),
        preferred_element_type=jnp.float32,
    )


def split(x):
    hi = x.astype(jnp.bfloat16)
    return hi, (x - hi.astype(jnp.float32)).astype(jnp.bfloat16)


def dot3(a, b):
    ah, al = a
    bh, bl = b

    def one(p, q):
        return jnp.dot(p, q, preferred_element_type=jnp.float32)

    return one(ah, bh) + (one(ah, bl) + one(al, bh))


def rows_of(pair, start, stop):
    return tuple(p[start:stop, :] for p in pair)


def columns_of(pair, start, stop):
    return tuple(p[:, start:stop] for p in pair)


def upper_pairs(n):
    return [(i, j) for i in range(n) for j in range(i, n)]


def masked(ref, count):
    rows = lax.broadcasted_iota(jnp.int32, ref.shape, 0)
    return jnp.where(rows < count, ref[...], 0.0)


def put_by_core(core, keep_ref, send_ref, half, place, tile):
    @pl.when(core == half)
    def _():
        keep_ref[place] = tile

    @pl.when(core != half)
    def _():
        send_ref[place] = tile


def overlaps_kernel(scalars, basis_ref, keep_ref, send_ref, *, weight):
    count, core = scalars[0], scalars[1]
    basis = masked(basis_ref, count)
    turned = split(jnp.transpose(basis * weight))
    basis = split(basis)
    m = basis_ref.shape[1] // BLOCK
    half_size = keep_ref.shape[0]
    position = 0
    for i in range(m):
        left = rows_of(turned, i * BLOCK, (i + 1) * BLOCK)
        own = dot3(left, columns_of(basis, i * BLOCK, m * BLOCK))
        rest = jnp.dot(
            left[1],
            basis[1][:, i * BLOCK : (i + 1) * BLOCK],
            preferred_element_type=jnp.float32,
        )
        tiles = [own[:, j * BLOCK : (j + 1) * BLOCK] for j in range(m - i)]
        tiles[0] = tiles[0] + rest
        for tile in tiles:
            put_by_core(
                core, keep_ref, send_ref, position // half_size, position % half_size, tile
            )
            position += 1


def products_kernel(scalars, basis_ref, block_ref, keep_ref, send_ref, *, weight):
    count, core = scalars[0], scalars[1]
    turned = split(jnp.transpose(masked(basis_ref, count) * weight))
    block = split(masked(block_ref, count))
    m, k = basis_ref.shape[1] // BLOCK, block_ref.shape[1] // BLOCK
    half_size = keep_ref.shape[0]
    for i in range(m):
        cross = dot3(rows_of(turned, i * BLOCK, (i + 1) * BLOCK), block)
        for j in range(k):
            position = i * k + j
            put_by_core(
                core, keep_ref, send_ref, position // half_size, position % half_size,
                cross[:, j * BLOCK : (j + 1) * BLOCK],
            )


def tile_of(core, own_ref, other_ref, position):
    half_size = own_ref.shape[0]
    here = core == position // half_size
    return jnp.where(here, own_ref[position % half_size], other_ref[position % half_size])


def defect_kernel(scalars, own_ref, other_ref, hi_ref, lo_ref):
    core = scalars[1]
    m = hi_ref.shape[0] // BLOCK
    eye = identity(BLOCK)
    for position, (i, j) in enumerate(upper_pairs(m)):
        tile = -tile_of(core, own_ref, other_ref, position)
        if i == j:
            tile = eye + tile
        rows, columns = slice(i * BLOCK, (i + 1) * BLOCK), slice(j * BLOCK, (j + 1) * BLOCK)
        hi_ref[rows, columns], lo_ref[rows, columns] = split(tile)
        if i != j:
            hi_ref[columns, rows], lo_ref[columns, rows] = split(jnp.transpose(tile))


def residual_kernel(
    scalars, own_ref, other_ref, hi_ref, lo_ref, basis_ref, block_ref,
    residual_ref, keep_ref, send_ref, *, weight
):
    count, core = scalars[0], scalars[1]
    m, k = basis_ref.shape[1] // BLOCK, block_ref.shape[1] // BLOCK
    coeffs = jnp.concatenate(
        [
            jnp.concatenate(
                [tile_of(core, own_ref, other_ref, i * k + j) for j in range(k)], axis=1
            )
            for i in range(m)
        ],
        axis=0,
    )
    total = coeffs + dot3((hi_ref[...], lo_ref[...]), split(coeffs))
    basis = masked(basis_ref, count)
    residual = masked(block_ref, count) - jnp.dot(
        basis, total, precision=HIGHEST, preferred_element_type=jnp.float32
    )
    residual_ref[...] = residual
    turned = split(jnp.transpose(residual * weight))
    residual = split(residual)
    half_size = keep_ref.shape[0]
    position = 0
    for i in range(k):
        row = dot3(
            rows_of(turned, i * BLOCK, (i + 1) * BLOCK), columns_of(residual, i * BLOCK, k * BLOCK)
        )
        for j in range(k - i):
            put_by_core(
                core, keep_ref, send_ref, position // half_size, position % half_size,
                row[:, j * BLOCK : (j + 1) * BLOCK],
            )
            position += 1


def dot3_nt(a, b):
    ah, al = a
    bh, bl = b

    def one(p, q):
        return lax.dot_general(p, q, (((1,), (1,)), ((), ())), preferred_element_type=jnp.float32)

    return one(ah, bh) + (one(ah, bl) + one(al, bh))


def factor_kernel(scalars, own_ref, other_ref, residual_ref, new_ref, factor_ref, w, inv_ref):
    size = residual_ref.shape[1]
    first = scalars[1] == 0
    half_size = own_ref.shape[0]
    zero = jnp.zeros((BLOCK, BLOCK), jnp.float32)
    for position, (i, j) in enumerate(upper_pairs(size // BLOCK)):
        swap = first if position < half_size else jnp.logical_not(first)
        w[i * BLOCK : (i + 1) * BLOCK, j * BLOCK : (j + 1) * BLOCK] = jnp.where(
            swap, own_ref[position % half_size], other_ref[position % half_size]
        )
        if i != j:
            w[j * BLOCK : (j + 1) * BLOCK, i * BLOCK : (i + 1) * BLOCK] = zero
    residual = split(residual_ref[...])
    zero = jnp.zeros((STEP, BLOCK), jnp.float32)
    lane = lax.broadcasted_iota(jnp.int32, (PANEL, BLOCK), 1)
    row = lax.broadcasted_iota(jnp.int32, (PANEL, BLOCK), 0)
    lanes = lax.broadcasted_iota(jnp.int32, (STEP, BLOCK), 1)
    rows = lax.broadcasted_iota(jnp.int32, (STEP, BLOCK), 0)
    following = None
    for k in range(size // STEP):
        o = k * STEP
        end = o + STEP
        lo = o // BLOCK * BLOCK
        hi = lo + BLOCK
        a0 = o - lo
        e0 = STEP - a0
        square = w[o:end, lo:hi] if following is None else following
        v = []
        for q in range(STEP // PANEL):
            eye = (lane - e0 == row + PANEL * q).astype(jnp.float32)
            inside = (lane >= a0) & (lane < a0 + STEP)
            v.append(jnp.where(inside, square[PANEL * q : PANEL * q + PANEL, :], eye))
        d = jnp.concatenate(eliminate(v, a0), axis=0)
        swapped = pltpu.roll(d, STEP, 1)
        here = (lanes >= a0) & (lanes < a0 + STEP)
        left4 = twice_left(jnp.where(here, swapped, d))
        if end < size:
            lo2 = end // BLOCK * BLOCK
            part = stacked_dot(left4, w[o:end, lo2 : lo2 + BLOCK])
            drop = stacked_dot_tn(part, part)[end - lo2 : end - lo2 + STEP, :]
            following = w[end : end + STEP, lo2 : lo2 + BLOCK] - drop
        z = stacked_dot(left4, w[o:end, :])
        z_here = z[:, lo:hi]
        upper = jnp.where(
            here & (lanes - a0 >= rows), d, jnp.where(lanes >= a0 + STEP, z_here, 0.0)
        )
        lower = jnp.where(
            here, jnp.where(lanes - a0 <= rows, swapped, 0.0), jnp.where(lanes < a0, z_here, 0.0)
        )
        for c in range(0, size, BLOCK):
            band = slice(c, c + BLOCK)
            factor_ref[o:end, band] = zero if c < lo else (upper if c == lo else z[:, band])
            inv_ref[o:end, band] = z[:, band] if c < lo else (lower if c == lo else zero)
        if end < size:
            pieces = [z[:, :lo]] if lo else []
            pieces.append(jnp.where(here, swapped, z_here))
            if hi < size:
                pieces.append(z[:, hi:])
            first_lane = end // BLOCK * BLOCK
            drop = stacked_dot_tn(z[:, first_lane:], jnp.concatenate(pieces, axis=1))
            column = lax.broadcasted_iota(jnp.int32, (size - end, size), 1)
            w[end:size, :] = (
                jnp.where((column >= o) & (column < end), 0.0, w[end:size, :])
                - drop[end - first_lane :, :]
            )
        if end == hi:
            new_ref[:, lo:hi] = dot3_nt(
                columns_of(residual, 0, hi), split(inv_ref[lo:hi, 0:hi])
            )


def call(kernel, out_shapes, scratch, name, dtype=jnp.float32):
    def run(scalars, *arrays):
        vmem = pl.BlockSpec(memory_space=pltpu.VMEM)
        return pl.pallas_call(
            kernel,
            out_shape=[jax.ShapeDtypeStruct(s, dtype) for s in out_shapes],
            in_specs=[pl.BlockSpec(memory_space=pltpu.SMEM)] + [vmem] * len(arrays),
            out_specs=[vmem] * len(out_shapes),
            scratch_shapes=scratch,
            compiler_params=pltpu.CompilerParams(vmem_limit_bytes=24 << 20),
            name=name,
        )(scalars, *arrays)

    return run


def swap_cores(x):
    return lax.ppermute(x, "row_2", [(0, 1), (1, 0)])


def exchange(x, axes):
    return lax.all_to_all(x, axes, 0, 0, tiled=True)


def to_all(x, axes):
    count = lax.axis_size(axes)
    return exchange(jnp.broadcast_to(x[None], (count, *x.shape)), axes)


def scattered(keep, send, near):
    total = (keep + swap_cores(send)).reshape(lax.axis_size(near), -1, 8, 128)
    return jnp.sum(exchange(total, near), axis=0)


def summed_by_pairs(part, axis):
    count = lax.axis_size(axis)
    step = 1
    while step < count:
        part = part + lax.ppermute(part, axis, [(i, i ^ step) for i in range(count)])
        step *= 2
    return part


def gathered(part, near, shape):
    whole = to_all(part, near).reshape(shape)
    return whole, swap_cores(whole)


def body(basis, block, counts):
    row_slots, size = block.shape
    m, k = basis.shape[1] // BLOCK, size // BLOCK
    devices = lax.axis_size(GRP) * lax.axis_size(ROW)
    weight = 1.0 / (row_slots * devices)
    scalars = jnp.stack([counts[0, 0], lax.axis_index("row_2").astype(jnp.int32)])
    overlap_half = (m * (m + 1) // 4, BLOCK, BLOCK)
    product_half = (m * k // 2, BLOCK, BLOCK)
    gram_half = (k * (k + 1) // 4, BLOCK, BLOCK)

    keep, send = call(
        functools.partial(overlaps_kernel, weight=weight), [overlap_half] * 2, [], "overlaps"
    )(scalars, basis)
    overlaps = scattered(keep, send, SLAB)
    keep, send = call(
        functools.partial(products_kernel, weight=weight), [product_half] * 2, [], "products"
    )(scalars, basis, block)
    products = scattered(keep, send, SLAB)
    overlaps = summed_by_pairs(overlaps, "grp_0")
    own, other = gathered(overlaps, SLAB, overlap_half)
    products = summed_by_pairs(products, "grp_0")
    own_product, other_product = gathered(products, SLAB, product_half)
    hi, lo = call(defect_kernel, [(m * BLOCK, m * BLOCK)] * 2, [], "defect", jnp.bfloat16)(
        scalars, own, other
    )
    residual, keep, send = call(
        functools.partial(residual_kernel, weight=weight),
        [block.shape, gram_half, gram_half],
        [],
        "residual",
    )(scalars, own_product, other_product, hi, lo, basis, block)

    part = scattered(keep, send, PLANE)
    part = jnp.sum(to_all(part, GRP), axis=0)
    own, other = gathered(part, PLANE, gram_half)
    new_block, factor = call(
        factor_kernel,
        [block.shape, (size, size)],
        [pltpu.VMEM((size, size), jnp.float32), pltpu.VMEM((size, size), jnp.float32)],
        "factor",
    )(scalars, own, other, residual)
    return new_block, factor


def solution(mesh):
    torus = Mesh(mesh.devices.reshape(mesh.shape["grp"] // 2, 2, 4, 4, 2), GRP_ROW)
    in_specs = (P(GRP_ROW, None), P(GRP_ROW, None), P(GRP, ROW))
    out_specs = (P(GRP_ROW, None), P())
    return jax.shard_map(body, mesh=torus, in_specs=in_specs, out_specs=out_specs, check_vma=False)
```

```python
import functools

import jax
import jax.numpy as jnp
from jax import lax
from jax.experimental import pallas as pl
from jax.experimental.pallas import tpu as pltpu
from jax.sharding import Mesh
from jax.sharding import PartitionSpec as P

ROW = ("row_0", "row_1", "row_2")
GRP = "grp"
GRP_ROW = (GRP, *ROW)
PLANE = ("row_0", "row_1")

BLOCK = 128
STEP = 64
PANEL = 8
HIGHEST = lax.Precision.HIGHEST


def identity(n):
    return (
        lax.broadcasted_iota(jnp.int32, (n, n), 0) == lax.broadcasted_iota(jnp.int32, (n, n), 1)
    ).astype(jnp.float32)


def spread(x):
    return jnp.broadcast_to(x, (PANEL, BLOCK))


def tree_sum(terms):
    while len(terms) > 1:
        terms = [a + b for a, b in zip(terms[::2], terms[1::2])]
    return terms[0]


def eliminate(v, a0):
    n = len(v)
    row = lax.broadcasted_iota(jnp.int32, (PANEL, BLOCK), 0)
    panel = range(PANEL)
    diag = [spread(v[0][:, a0 + j : a0 + j + 1]) for j in panel]
    for p in range(n):
        base = a0 + PANEL * p
        turned = {
            q: [spread(v[q][:, base + j : base + j + 1]) for j in panel] for q in range(p + 1, n)
        }
        if p + 1 < n:
            after = base + PANEL
            ahead = [spread(v[p + 1][:, after + j : after + j + 1]) for j in panel]
        current = v[p]
        rows, coefs, inverses = [], [], []
        scale = None
        for k in panel:
            inv = lax.rsqrt(spread(diag[k][k : k + 1, :]))
            col = diag[k] * inv
            r = [spread(col[j : j + 1, :]) if j > k else None for j in panel]
            for j in range(k + 1, PANEL):
                diag[j] = diag[j] - col * r[j]
            own = spread(current[k : k + 1, :]) * inv
            rows.append(own)
            if k < PANEL - 1:
                current = current - jnp.where(row > k, col, 0.0) * own
            scale = inv if scale is None else jnp.where(row >= k, inv, scale)
            coefs.append(r)
            inverses.append(inv)
        v[p] = current * scale
        for q in range(p + 1, n):
            t = turned[q]
            for k in panel:
                t[k] = t[k] * inverses[k]
                for j in range(k + 1, PANEL):
                    t[j] = t[j] - t[k] * coefs[k][j]
            v[q] = v[q] - tree_sum([t[k] * rows[k] for k in panel])
            if q == p + 1:
                diag = [
                    ahead[j] - tree_sum([t[k] * spread(t[k][j : j + 1, :]) for k in panel])
                    for j in panel
                ]
    return v


def twice_left(x):
    hi, lo = split(x)
    lane = lax.broadcasted_iota(jnp.int32, x.shape, 1)
    both = jnp.where(lane < STEP, hi.astype(jnp.float32), lo.astype(jnp.float32))
    both = both.astype(jnp.bfloat16)
    return jnp.concatenate([both, both], axis=1)


def stacked_dot(left4, x):
    hi, lo = split(x)
    return jnp.dot(
        left4, jnp.concatenate([hi, hi, lo, lo], axis=0), preferred_element_type=jnp.float32
    )


def stacked_dot_tn(a, b):
    ah, al = split(a)
    bh, bl = split(b)
    return lax.dot_general(
        jnp.concatenate([ah, al, ah, al], axis=0),
        jnp.concatenate([bh, bh, bl, bl], axis=0),
        (((0,), (0,)), ((), ())),
        preferred_element_type=jnp.float32,
    )


def split(x):
    hi = x.astype(jnp.bfloat16)
    return hi, (x - hi.astype(jnp.float32)).astype(jnp.bfloat16)


def dot3(a, b):
    ah, al = a
    bh, bl = b

    def one(p, q):
        return jnp.dot(p, q, preferred_element_type=jnp.float32)

    return one(ah, bh) + (one(ah, bl) + one(al, bh))


def rows_of(pair, start, stop):
    return tuple(p[start:stop, :] for p in pair)


def columns_of(pair, start, stop):
    return tuple(p[:, start:stop] for p in pair)


def upper_pairs(n):
    return [(i, j) for i in range(n) for j in range(i, n)]


def masked(ref, count):
    rows = lax.broadcasted_iota(jnp.int32, ref.shape, 0)
    return jnp.where(rows < count, ref[...], 0.0)


def put_by_core(core, keep_ref, send_ref, half, place, tile):
    @pl.when(core == half)
    def _():
        keep_ref[place] = tile

    @pl.when(core != half)
    def _():
        send_ref[place] = tile


def products_kernel(scalars, basis_ref, block_ref, keep_ref, send_ref, *, weight):
    count, core = scalars[0], scalars[1]
    basis = masked(basis_ref, count)
    block = masked(block_ref, count)
    turned = split(jnp.transpose(basis * weight))
    basis = split(basis)
    block = split(block)
    m, k = basis_ref.shape[1] // BLOCK, block_ref.shape[1] // BLOCK
    half_size = keep_ref.shape[0]
    position = 0
    for i in range(m):
        left = rows_of(turned, i * BLOCK, (i + 1) * BLOCK)
        own = dot3(left, columns_of(basis, i * BLOCK, m * BLOCK))
        cross = dot3(left, block)
        rest = jnp.dot(
            left[1],
            basis[1][:, i * BLOCK : (i + 1) * BLOCK],
            preferred_element_type=jnp.float32,
        )
        tiles = [own[:, j * BLOCK : (j + 1) * BLOCK] for j in range(m - i)]
        tiles[0] = tiles[0] + rest
        tiles += [cross[:, j * BLOCK : (j + 1) * BLOCK] for j in range(k)]
        for tile in tiles:
            put_by_core(
                core, keep_ref, send_ref, position // half_size, position % half_size, tile
            )
            position += 1


def residual_kernel(
    scalars, own_ref, other_ref, basis_ref, block_ref, residual_ref, keep_ref, send_ref,
    s_hi, s_lo, *, weight
):
    count, core = scalars[0], scalars[1]
    m, k = basis_ref.shape[1] // BLOCK, block_ref.shape[1] // BLOCK
    half_size = own_ref.shape[0]
    first = core == 0

    def tile_at(position):
        mine, theirs = own_ref[position % half_size], other_ref[position % half_size]
        swap = first if position < half_size else jnp.logical_not(first)
        return jnp.where(swap, mine, theirs)

    position = 0
    coeffs = []
    eye = identity(BLOCK)
    for i in range(m):
        for j in range(i, m):
            tile = -tile_at(position)
            position += 1
            if i == j:
                tile = eye + tile
            hi, lo = split(tile)
            s_hi[i * BLOCK : (i + 1) * BLOCK, j * BLOCK : (j + 1) * BLOCK] = hi
            s_lo[i * BLOCK : (i + 1) * BLOCK, j * BLOCK : (j + 1) * BLOCK] = lo
            if i != j:
                hi, lo = split(jnp.transpose(tile))
                s_hi[j * BLOCK : (j + 1) * BLOCK, i * BLOCK : (i + 1) * BLOCK] = hi
                s_lo[j * BLOCK : (j + 1) * BLOCK, i * BLOCK : (i + 1) * BLOCK] = lo
        row = []
        for j in range(k):
            row.append(tile_at(position))
            position += 1
        coeffs.append(jnp.concatenate(row, axis=1))
    coeffs = jnp.concatenate(coeffs, axis=0)
    total = coeffs + dot3((s_hi[...], s_lo[...]), split(coeffs))
    basis = masked(basis_ref, count)
    residual = masked(block_ref, count) - jnp.dot(
        basis, total, precision=HIGHEST, preferred_element_type=jnp.float32
    )
    residual_ref[...] = residual
    turned = split(jnp.transpose(residual * weight))
    residual = split(residual)
    half_size = keep_ref.shape[0]
    position = 0
    for i in range(k):
        row = dot3(
            rows_of(turned, i * BLOCK, (i + 1) * BLOCK), columns_of(residual, i * BLOCK, k * BLOCK)
        )
        for j in range(k - i):
            put_by_core(
                core, keep_ref, send_ref, position // half_size, position % half_size,
                row[:, j * BLOCK : (j + 1) * BLOCK],
            )
            position += 1


def dot3_nt(a, b):
    ah, al = a
    bh, bl = b

    def one(p, q):
        return lax.dot_general(p, q, (((1,), (1,)), ((), ())), preferred_element_type=jnp.float32)

    return one(ah, bh) + (one(ah, bl) + one(al, bh))


def factor_kernel(scalars, own_ref, other_ref, residual_ref, new_ref, factor_ref, w, inv_ref):
    size = residual_ref.shape[1]
    first = scalars[1] == 0
    half_size = own_ref.shape[0]
    zero = jnp.zeros((BLOCK, BLOCK), jnp.float32)
    for position, (i, j) in enumerate(upper_pairs(size // BLOCK)):
        swap = first if position < half_size else jnp.logical_not(first)
        w[i * BLOCK : (i + 1) * BLOCK, j * BLOCK : (j + 1) * BLOCK] = jnp.where(
            swap, own_ref[position % half_size], other_ref[position % half_size]
        )
        if i != j:
            w[j * BLOCK : (j + 1) * BLOCK, i * BLOCK : (i + 1) * BLOCK] = zero
    residual = split(residual_ref[...])
    zero = jnp.zeros((STEP, BLOCK), jnp.float32)
    lane = lax.broadcasted_iota(jnp.int32, (PANEL, BLOCK), 1)
    row = lax.broadcasted_iota(jnp.int32, (PANEL, BLOCK), 0)
    lanes = lax.broadcasted_iota(jnp.int32, (STEP, BLOCK), 1)
    rows = lax.broadcasted_iota(jnp.int32, (STEP, BLOCK), 0)
    following = None
    for k in range(size // STEP):
        o = k * STEP
        end = o + STEP
        lo = o // BLOCK * BLOCK
        hi = lo + BLOCK
        a0 = o - lo
        e0 = STEP - a0
        square = w[o:end, lo:hi] if following is None else following
        v = []
        for q in range(STEP // PANEL):
            eye = (lane - e0 == row + PANEL * q).astype(jnp.float32)
            inside = (lane >= a0) & (lane < a0 + STEP)
            v.append(jnp.where(inside, square[PANEL * q : PANEL * q + PANEL, :], eye))
        d = jnp.concatenate(eliminate(v, a0), axis=0)
        swapped = pltpu.roll(d, STEP, 1)
        here = (lanes >= a0) & (lanes < a0 + STEP)
        left4 = twice_left(jnp.where(here, swapped, d))
        if end < size:
            lo2 = end // BLOCK * BLOCK
            part = stacked_dot(left4, w[o:end, lo2 : lo2 + BLOCK])
            drop = stacked_dot_tn(part, part)[end - lo2 : end - lo2 + STEP, :]
            following = w[end : end + STEP, lo2 : lo2 + BLOCK] - drop
        z = stacked_dot(left4, w[o:end, :])
        z_here = z[:, lo:hi]
        upper = jnp.where(
            here & (lanes - a0 >= rows), d, jnp.where(lanes >= a0 + STEP, z_here, 0.0)
        )
        lower = jnp.where(
            here, jnp.where(lanes - a0 <= rows, swapped, 0.0), jnp.where(lanes < a0, z_here, 0.0)
        )
        for c in range(0, size, BLOCK):
            band = slice(c, c + BLOCK)
            factor_ref[o:end, band] = zero if c < lo else (upper if c == lo else z[:, band])
            inv_ref[o:end, band] = z[:, band] if c < lo else (lower if c == lo else zero)
        if end < size:
            pieces = [z[:, :lo]] if lo else []
            pieces.append(jnp.where(here, swapped, z_here))
            if hi < size:
                pieces.append(z[:, hi:])
            first_lane = end // BLOCK * BLOCK
            drop = stacked_dot_tn(z[:, first_lane:], jnp.concatenate(pieces, axis=1))
            column = lax.broadcasted_iota(jnp.int32, (size - end, size), 1)
            w[end:size, :] = (
                jnp.where((column >= o) & (column < end), 0.0, w[end:size, :])
                - drop[end - first_lane :, :]
            )
        if end == hi:
            new_ref[:, lo:hi] = dot3_nt(
                columns_of(residual, 0, hi), split(inv_ref[lo:hi, 0:hi])
            )


def call(kernel, out_shapes, scratch, name):
    def run(scalars, *arrays):
        vmem = pl.BlockSpec(memory_space=pltpu.VMEM)
        return pl.pallas_call(
            kernel,
            out_shape=[jax.ShapeDtypeStruct(s, jnp.float32) for s in out_shapes],
            in_specs=[pl.BlockSpec(memory_space=pltpu.SMEM)] + [vmem] * len(arrays),
            out_specs=[vmem] * len(out_shapes),
            scratch_shapes=scratch,
            compiler_params=pltpu.CompilerParams(vmem_limit_bytes=48 << 20),
            name=name,
        )(scalars, *arrays)

    return run


def swap_cores(x):
    return lax.ppermute(x, "row_2", [(0, 1), (1, 0)])


def exchange(x, axes):
    return lax.all_to_all(x, axes, 0, 0, tiled=True)


def to_all(x, axes):
    count = lax.axis_size(axes)
    return exchange(jnp.broadcast_to(x[None], (count, *x.shape)), axes)


def crossed_lines():
    nx, ny = lax.axis_size("row_0"), lax.axis_size("row_1")

    def at(x, y, core):
        return (x * ny + y) * 2 + core

    first = [[at(x, y, 0) for x in range(nx)] for y in range(ny)]
    second = [[at(x, y, 1) for y in range(ny)] for x in range(nx)]
    return first + second


def crossed_sheets():
    nz, nx, ny = lax.axis_size(GRP), lax.axis_size("row_0"), lax.axis_size("row_1")

    def at(z, x, y, core):
        return ((z * nx + x) * ny + y) * 2 + core

    first = [[at(z, x, y, 0) for z in range(nz) for y in range(ny)] for x in range(nx)]
    second = [[at(z, x, y, 1) for z in range(nz) for x in range(nx)] for y in range(ny)]
    return first + second


def exchange_in(x, axes, groups):
    return lax.all_to_all(x, axes, 0, 0, axis_index_groups=groups, tiled=True)


def sum_crossed(keep, send):
    lines, sheets = crossed_lines(), crossed_sheets()
    total = (keep + swap_cores(send)).reshape(len(lines[0]), -1, 8, 128)
    part = jnp.sum(exchange_in(total, ROW, lines), axis=0)
    size, count = part.shape[0], len(sheets[0])
    part = jnp.pad(part, ((0, -size % count), (0, 0), (0, 0)))
    part = part.reshape(count, -1, 8, 128)
    part = jnp.sum(exchange_in(part, GRP_ROW, sheets), axis=0)
    part = exchange_in(jnp.broadcast_to(part[None], (count, *part.shape)), GRP_ROW, sheets)
    part = part.reshape(-1, 8, 128)[:size]
    whole = jnp.broadcast_to(part[None], (len(lines[0]), *part.shape))
    whole = exchange_in(whole, ROW, lines).reshape(keep.shape)
    return whole, swap_cores(whole)


def sum_halves(keep, send, near, far):
    total = (keep + swap_cores(send)).reshape(lax.axis_size(near), -1, 8, 128)
    part = jnp.sum(exchange(total, near), axis=0)
    part = jnp.sum(to_all(part, far), axis=0)
    whole = to_all(part, near).reshape(keep.shape)
    return whole, swap_cores(whole)


def body(basis, block, counts):
    row_slots, size = block.shape
    m, k = basis.shape[1] // BLOCK, size // BLOCK
    devices = lax.axis_size(GRP) * lax.axis_size(ROW)
    weight = 1.0 / (row_slots * devices)
    scalars = jnp.stack([counts[0, 0], lax.axis_index("row_2").astype(jnp.int32)])
    tiles = (m * (m + 1) // 2 + m * k) // 2
    gram_tiles = k * (k + 1) // 4
    half = (tiles, BLOCK, BLOCK)
    gram_half = (gram_tiles, BLOCK, BLOCK)
    keep, send = call(
        functools.partial(products_kernel, weight=weight), [half, half], [], "products"
    )(scalars, basis, block)
    own, other = sum_crossed(keep, send)
    wide = pltpu.VMEM((m * BLOCK, m * BLOCK), jnp.bfloat16)
    residual, keep, send = call(
        functools.partial(residual_kernel, weight=weight),
        [block.shape, gram_half, gram_half],
        [wide, wide],
        "residual",
    )(scalars, own, other, basis, block)
    own, other = sum_halves(keep, send, PLANE, GRP)
    new_block, factor = call(
        factor_kernel,
        [block.shape, (size, size)],
        [
            pltpu.VMEM((size, size), jnp.float32),
            pltpu.VMEM((size, size), jnp.float32),
        ],
        "factor",
    )(scalars, own, other, residual)
    return new_block, factor


def solution(mesh):
    torus = Mesh(mesh.devices.reshape(mesh.shape["grp"], 4, 4, 2), GRP_ROW)
    in_specs = (P(GRP_ROW, None), P(GRP_ROW, None), P(GRP, ROW))
    out_specs = (P(GRP_ROW, None), P())
    return jax.shard_map(body, mesh=torus, in_specs=in_specs, out_specs=out_specs, check_vma=False)
```

```python
import functools

import jax
import jax.numpy as jnp
from jax import lax
from jax.experimental import pallas as pl
from jax.experimental.pallas import tpu as pltpu
from jax.sharding import Mesh
from jax.sharding import PartitionSpec as P

ROW = ("row_0", "row_1", "row_2")
GRP = ("grp_0", "grp_1")
GRP_ROW = (*GRP, *ROW)
PLANE = ("row_0", "row_1")
SLAB = ("grp_1", "row_0", "row_1")

BLOCK = 128
STEP = 64
PANEL = 8
HIGHEST = lax.Precision.HIGHEST


def identity(n):
    return (
        lax.broadcasted_iota(jnp.int32, (n, n), 0) == lax.broadcasted_iota(jnp.int32, (n, n), 1)
    ).astype(jnp.float32)


def spread(x):
    return jnp.broadcast_to(x, (PANEL, BLOCK))


def tree_sum(terms):
    while len(terms) > 1:
        terms = [a + b for a, b in zip(terms[::2], terms[1::2])]
    return terms[0]


def eliminate(v, a0):
    n = len(v)
    row = lax.broadcasted_iota(jnp.int32, (PANEL, BLOCK), 0)
    panel = range(PANEL)
    diag = [spread(v[0][:, a0 + j : a0 + j + 1]) for j in panel]
    for p in range(n):
        base = a0 + PANEL * p
        turned = {
            q: [spread(v[q][:, base + j : base + j + 1]) for j in panel] for q in range(p + 1, n)
        }
        if p + 1 < n:
            after = base + PANEL
            ahead = [spread(v[p + 1][:, after + j : after + j + 1]) for j in panel]
        current = v[p]
        rows, coefs, inverses = [], [], []
        scale = None
        for k in panel:
            inv = lax.rsqrt(spread(diag[k][k : k + 1, :]))
            col = diag[k] * inv
            r = [spread(col[j : j + 1, :]) if j > k else None for j in panel]
            for j in range(k + 1, PANEL):
                diag[j] = diag[j] - col * r[j]
            own = spread(current[k : k + 1, :]) * inv
            rows.append(own)
            if k < PANEL - 1:
                current = current - jnp.where(row > k, col, 0.0) * own
            scale = inv if scale is None else jnp.where(row >= k, inv, scale)
            coefs.append(r)
            inverses.append(inv)
        v[p] = current * scale
        for q in range(p + 1, n):
            t = turned[q]
            for k in panel:
                t[k] = t[k] * inverses[k]
                for j in range(k + 1, PANEL):
                    t[j] = t[j] - t[k] * coefs[k][j]
            v[q] = v[q] - tree_sum([t[k] * rows[k] for k in panel])
            if q == p + 1:
                diag = [
                    ahead[j] - tree_sum([t[k] * spread(t[k][j : j + 1, :]) for k in panel])
                    for j in panel
                ]
    return v


def twice_left(x):
    hi, lo = split(x)
    lane = lax.broadcasted_iota(jnp.int32, x.shape, 1)
    both = jnp.where(lane < STEP, hi.astype(jnp.float32), lo.astype(jnp.float32))
    both = both.astype(jnp.bfloat16)
    return jnp.concatenate([both, both], axis=1)


def stacked_dot(left4, x):
    hi, lo = split(x)
    return jnp.dot(
        left4, jnp.concatenate([hi, hi, lo, lo], axis=0), preferred_element_type=jnp.float32
    )


def stacked_dot_tn(a, b):
    ah, al = split(a)
    bh, bl = split(b)
    return lax.dot_general(
        jnp.concatenate([ah, al, ah, al], axis=0),
        jnp.concatenate([bh, bh, bl, bl], axis=0),
        (((0,), (0,)), ((), ())),
        preferred_element_type=jnp.float32,
    )


def split(x):
    hi = x.astype(jnp.bfloat16)
    return hi, (x - hi.astype(jnp.float32)).astype(jnp.bfloat16)


def dot3(a, b):
    ah, al = a
    bh, bl = b

    def one(p, q):
        return jnp.dot(p, q, preferred_element_type=jnp.float32)

    return one(ah, bh) + (one(ah, bl) + one(al, bh))


def rows_of(pair, start, stop):
    return tuple(p[start:stop, :] for p in pair)


def columns_of(pair, start, stop):
    return tuple(p[:, start:stop] for p in pair)


def upper_pairs(n):
    return [(i, j) for i in range(n) for j in range(i, n)]


def masked(ref, count):
    rows = lax.broadcasted_iota(jnp.int32, ref.shape, 0)
    return jnp.where(rows < count, ref[...], 0.0)


def products_kernel(scalars, basis_ref, block_ref, keep_ref, send_ref, all_ref, *, weight):
    count, core = scalars[0], scalars[1]
    basis = masked(basis_ref, count)
    block = masked(block_ref, count)
    turned = split(jnp.transpose(basis * weight))
    basis = split(basis)
    block = split(block)
    m, k = basis_ref.shape[1] // BLOCK, block_ref.shape[1] // BLOCK
    half_size = keep_ref.shape[0]
    position = 0
    for i in range(m):
        left = rows_of(turned, i * BLOCK, (i + 1) * BLOCK)
        own = dot3(left, columns_of(basis, i * BLOCK, m * BLOCK))
        cross = dot3(left, block)
        rest = jnp.dot(
            left[1],
            basis[1][:, i * BLOCK : (i + 1) * BLOCK],
            preferred_element_type=jnp.float32,
        )
        tiles = [own[:, j * BLOCK : (j + 1) * BLOCK] for j in range(m - i)]
        tiles[0] = tiles[0] + rest
        tiles += [cross[:, j * BLOCK : (j + 1) * BLOCK] for j in range(k)]
        for tile in tiles:
            all_ref[position] = tile
            position += 1
    keep_ref[...] = all_ref[pl.ds(core * half_size, half_size)]
    send_ref[...] = all_ref[pl.ds((1 - core) * half_size, half_size)]


def residual_kernel(
    scalars, own_ref, other_ref, basis_ref, block_ref, residual_ref, keep_ref, send_ref,
    s_hi, s_lo, gram_ref, *, weight
):
    count, core = scalars[0], scalars[1]
    m, k = basis_ref.shape[1] // BLOCK, block_ref.shape[1] // BLOCK
    half_size = own_ref.shape[0]
    first = core == 0

    def tile_at(position):
        mine, theirs = own_ref[position % half_size], other_ref[position % half_size]
        swap = first if position < half_size else jnp.logical_not(first)
        return jnp.where(swap, mine, theirs)

    position = 0
    coeffs = []
    eye = identity(BLOCK)
    for i in range(m):
        for j in range(i, m):
            tile = -tile_at(position)
            position += 1
            if i == j:
                tile = eye + tile
            hi, lo = split(tile)
            s_hi[i * BLOCK : (i + 1) * BLOCK, j * BLOCK : (j + 1) * BLOCK] = hi
            s_lo[i * BLOCK : (i + 1) * BLOCK, j * BLOCK : (j + 1) * BLOCK] = lo
            if i != j:
                hi, lo = split(jnp.transpose(tile))
                s_hi[j * BLOCK : (j + 1) * BLOCK, i * BLOCK : (i + 1) * BLOCK] = hi
                s_lo[j * BLOCK : (j + 1) * BLOCK, i * BLOCK : (i + 1) * BLOCK] = lo
        row = []
        for j in range(k):
            row.append(tile_at(position))
            position += 1
        coeffs.append(jnp.concatenate(row, axis=1))
    coeffs = jnp.concatenate(coeffs, axis=0)
    total = coeffs + dot3((s_hi[...], s_lo[...]), split(coeffs))
    basis = masked(basis_ref, count)
    residual = masked(block_ref, count) - jnp.dot(
        basis, total, precision=HIGHEST, preferred_element_type=jnp.float32
    )
    residual_ref[...] = residual
    turned = split(jnp.transpose(residual * weight))
    residual = split(residual)
    half_size = keep_ref.shape[0]
    position = 0
    for i in range(k):
        row = dot3(
            rows_of(turned, i * BLOCK, (i + 1) * BLOCK), columns_of(residual, i * BLOCK, k * BLOCK)
        )
        for j in range(k - i):
            gram_ref[position] = row[:, j * BLOCK : (j + 1) * BLOCK]
            position += 1
    keep_ref[...] = gram_ref[pl.ds(core * half_size, half_size)]
    send_ref[...] = gram_ref[pl.ds((1 - core) * half_size, half_size)]


def dot3_nt(a, b):
    ah, al = a
    bh, bl = b

    def one(p, q):
        return lax.dot_general(p, q, (((1,), (1,)), ((), ())), preferred_element_type=jnp.float32)

    return one(ah, bh) + (one(ah, bl) + one(al, bh))


def factor_kernel(scalars, own_ref, other_ref, residual_ref, new_ref, factor_ref, w, inv_ref):
    size = residual_ref.shape[1]
    first = scalars[1] == 0
    half_size = own_ref.shape[0]
    zero = jnp.zeros((BLOCK, BLOCK), jnp.float32)
    for position, (i, j) in enumerate(upper_pairs(size // BLOCK)):
        swap = first if position < half_size else jnp.logical_not(first)
        w[i * BLOCK : (i + 1) * BLOCK, j * BLOCK : (j + 1) * BLOCK] = jnp.where(
            swap, own_ref[position % half_size], other_ref[position % half_size]
        )
        if i != j:
            w[j * BLOCK : (j + 1) * BLOCK, i * BLOCK : (i + 1) * BLOCK] = zero
    residual = split(residual_ref[...])
    zero = jnp.zeros((STEP, BLOCK), jnp.float32)
    lane = lax.broadcasted_iota(jnp.int32, (PANEL, BLOCK), 1)
    row = lax.broadcasted_iota(jnp.int32, (PANEL, BLOCK), 0)
    lanes = lax.broadcasted_iota(jnp.int32, (STEP, BLOCK), 1)
    rows = lax.broadcasted_iota(jnp.int32, (STEP, BLOCK), 0)
    following = None
    for k in range(size // STEP):
        o = k * STEP
        end = o + STEP
        lo = o // BLOCK * BLOCK
        hi = lo + BLOCK
        a0 = o - lo
        e0 = STEP - a0
        square = w[o:end, lo:hi] if following is None else following
        v = []
        for q in range(STEP // PANEL):
            eye = (lane - e0 == row + PANEL * q).astype(jnp.float32)
            inside = (lane >= a0) & (lane < a0 + STEP)
            v.append(jnp.where(inside, square[PANEL * q : PANEL * q + PANEL, :], eye))
        d = jnp.concatenate(eliminate(v, a0), axis=0)
        swapped = pltpu.roll(d, STEP, 1)
        here = (lanes >= a0) & (lanes < a0 + STEP)
        left4 = twice_left(jnp.where(here, swapped, d))
        if end < size:
            lo2 = end // BLOCK * BLOCK
            part = stacked_dot(left4, w[o:end, lo2 : lo2 + BLOCK])
            drop = stacked_dot_tn(part, part)[end - lo2 : end - lo2 + STEP, :]
            following = w[end : end + STEP, lo2 : lo2 + BLOCK] - drop
        z = stacked_dot(left4, w[o:end, :])
        z_here = z[:, lo:hi]
        upper = jnp.where(
            here & (lanes - a0 >= rows), d, jnp.where(lanes >= a0 + STEP, z_here, 0.0)
        )
        lower = jnp.where(
            here, jnp.where(lanes - a0 <= rows, swapped, 0.0), jnp.where(lanes < a0, z_here, 0.0)
        )
        for c in range(0, size, BLOCK):
            band = slice(c, c + BLOCK)
            factor_ref[o:end, band] = zero if c < lo else (upper if c == lo else z[:, band])
            inv_ref[o:end, band] = z[:, band] if c < lo else (lower if c == lo else zero)
        if end < size:
            pieces = [z[:, :lo]] if lo else []
            pieces.append(jnp.where(here, swapped, z_here))
            if hi < size:
                pieces.append(z[:, hi:])
            first_lane = end // BLOCK * BLOCK
            drop = stacked_dot_tn(z[:, first_lane:], jnp.concatenate(pieces, axis=1))
            column = lax.broadcasted_iota(jnp.int32, (size - end, size), 1)
            w[end:size, :] = (
                jnp.where((column >= o) & (column < end), 0.0, w[end:size, :])
                - drop[end - first_lane :, :]
            )
        if end == hi:
            new_ref[:, lo:hi] = dot3_nt(
                columns_of(residual, 0, hi), split(inv_ref[lo:hi, 0:hi])
            )


def call(kernel, out_shapes, scratch, name):
    def run(scalars, *arrays):
        vmem = pl.BlockSpec(memory_space=pltpu.VMEM)
        return pl.pallas_call(
            kernel,
            out_shape=[jax.ShapeDtypeStruct(s, jnp.float32) for s in out_shapes],
            in_specs=[pl.BlockSpec(memory_space=pltpu.SMEM)] + [vmem] * len(arrays),
            out_specs=[vmem] * len(out_shapes),
            scratch_shapes=scratch,
            compiler_params=pltpu.CompilerParams(vmem_limit_bytes=24 << 20),
            name=name,
        )(scalars, *arrays)

    return run


def swap_cores(x):
    return lax.ppermute(x, "row_2", [(0, 1), (1, 0)])


def exchange(x, axes):
    return lax.all_to_all(x, axes, 0, 0, tiled=True)


def to_all(x, axes):
    count = lax.axis_size(axes)
    return exchange(jnp.broadcast_to(x[None], (count, *x.shape)), axes)


def sum_halves(keep, send, near, far):
    total = (keep + swap_cores(send)).reshape(lax.axis_size(near), -1, 8, 128)
    part = jnp.sum(exchange(total, near), axis=0)
    part = jnp.sum(to_all(part, far), axis=0)
    whole = to_all(part, near).reshape(keep.shape)
    return whole, swap_cores(whole)


def body(basis, block, counts):
    row_slots, size = block.shape
    m, k = basis.shape[1] // BLOCK, size // BLOCK
    devices = lax.axis_size(GRP) * lax.axis_size(ROW)
    weight = 1.0 / (row_slots * devices)
    scalars = jnp.stack([counts[0, 0], lax.axis_index("row_2").astype(jnp.int32)])
    tiles = (m * (m + 1) // 2 + m * k) // 2
    gram_tiles = k * (k + 1) // 4
    half = (tiles, BLOCK, BLOCK)
    gram_half = (gram_tiles, BLOCK, BLOCK)
    keep, send = call(
        functools.partial(products_kernel, weight=weight), [half, half],
        [pltpu.VMEM((2 * tiles, BLOCK, BLOCK), jnp.float32)], "products"
    )(scalars, basis, block)
    own, other = sum_halves(keep, send, SLAB, "grp_0")
    wide = pltpu.VMEM((m * BLOCK, m * BLOCK), jnp.bfloat16)
    residual, keep, send = call(
        functools.partial(residual_kernel, weight=weight),
        [block.shape, gram_half, gram_half],
        [wide, wide, pltpu.VMEM((2 * gram_tiles, BLOCK, BLOCK), jnp.float32)],
        "residual",
    )(scalars, own, other, basis, block)
    own, other = sum_halves(keep, send, PLANE, GRP)
    new_block, factor = call(
        factor_kernel,
        [block.shape, (size, size)],
        [
            pltpu.VMEM((size, size), jnp.float32),
            pltpu.VMEM((size, size), jnp.float32),
        ],
        "factor",
    )(scalars, own, other, residual)
    return new_block, factor


def solution(mesh):
    torus = Mesh(mesh.devices.reshape(mesh.shape["grp"] // 2, 2, 4, 4, 2), GRP_ROW)
    in_specs = (P(GRP_ROW, None), P(GRP_ROW, None), P(GRP, ROW))
    out_specs = (P(GRP_ROW, None), P())
    return jax.shard_map(body, mesh=torus, in_specs=in_specs, out_specs=out_specs, check_vma=False)
```

```python
import functools

import jax
import jax.numpy as jnp
from jax import lax
from jax.experimental import pallas as pl
from jax.experimental.pallas import tpu as pltpu
from jax.sharding import Mesh
from jax.sharding import PartitionSpec as P

ROW = ("row_0", "row_1", "row_2")
GRP = ("grp_0", "grp_1")
GRP_ROW = (*GRP, *ROW)
PLANE = ("row_0", "row_1")
SLAB = ("grp_1", "row_0", "row_1")

BLOCK = 128
STEP = 64
PANEL = 8
HIGHEST = lax.Precision.HIGHEST


def identity(n):
    return (
        lax.broadcasted_iota(jnp.int32, (n, n), 0) == lax.broadcasted_iota(jnp.int32, (n, n), 1)
    ).astype(jnp.float32)


def spread(x):
    return jnp.broadcast_to(x, (PANEL, BLOCK))


def tree_sum(terms):
    while len(terms) > 1:
        terms = [a + b for a, b in zip(terms[::2], terms[1::2])]
    return terms[0]


def eliminate(v, a0):
    n = len(v)
    row = lax.broadcasted_iota(jnp.int32, (PANEL, BLOCK), 0)
    panel = range(PANEL)
    diag = [spread(v[0][:, a0 + j : a0 + j + 1]) for j in panel]
    for p in range(n):
        base = a0 + PANEL * p
        turned = {
            q: [spread(v[q][:, base + j : base + j + 1]) for j in panel] for q in range(p + 1, n)
        }
        if p + 1 < n:
            after = base + PANEL
            ahead = [spread(v[p + 1][:, after + j : after + j + 1]) for j in panel]
        current = v[p]
        rows, coefs, inverses = [], [], []
        scale = None
        for k in panel:
            inv = lax.rsqrt(spread(diag[k][k : k + 1, :]))
            col = diag[k] * inv
            r = [spread(col[j : j + 1, :]) if j > k else None for j in panel]
            for j in range(k + 1, PANEL):
                diag[j] = diag[j] - col * r[j]
            own = spread(current[k : k + 1, :]) * inv
            rows.append(own)
            if k < PANEL - 1:
                current = current - jnp.where(row > k, col, 0.0) * own
            scale = inv if scale is None else jnp.where(row >= k, inv, scale)
            coefs.append(r)
            inverses.append(inv)
        v[p] = current * scale
        for q in range(p + 1, n):
            t = turned[q]
            for k in panel:
                t[k] = t[k] * inverses[k]
                for j in range(k + 1, PANEL):
                    t[j] = t[j] - t[k] * coefs[k][j]
            v[q] = v[q] - tree_sum([t[k] * rows[k] for k in panel])
            if q == p + 1:
                diag = [
                    ahead[j] - tree_sum([t[k] * spread(t[k][j : j + 1, :]) for k in panel])
                    for j in panel
                ]
    return v


def twice_left(x):
    hi, lo = split(x)
    lane = lax.broadcasted_iota(jnp.int32, x.shape, 1)
    both = jnp.where(lane < STEP, hi.astype(jnp.float32), lo.astype(jnp.float32))
    both = both.astype(jnp.bfloat16)
    return jnp.concatenate([both, both], axis=1)


def stacked_dot(left4, x):
    hi, lo = split(x)
    return jnp.dot(
        left4, jnp.concatenate([hi, hi, lo, lo], axis=0), preferred_element_type=jnp.float32
    )


def stacked_dot_tn(a, b):
    ah, al = split(a)
    bh, bl = split(b)
    return lax.dot_general(
        jnp.concatenate([ah, al, ah, al], axis=0),
        jnp.concatenate([bh, bh, bl, bl], axis=0),
        (((0,), (0,)), ((), ())),
        preferred_element_type=jnp.float32,
    )


def split(x):
    hi = x.astype(jnp.bfloat16)
    return hi, (x - hi.astype(jnp.float32)).astype(jnp.bfloat16)


def dot3(a, b):
    ah, al = a
    bh, bl = b

    def one(p, q):
        return jnp.dot(p, q, preferred_element_type=jnp.float32)

    return one(ah, bh) + (one(ah, bl) + one(al, bh))


def rows_of(pair, start, stop):
    return tuple(p[start:stop, :] for p in pair)


def columns_of(pair, start, stop):
    return tuple(p[:, start:stop] for p in pair)


def upper_pairs(n):
    return [(i, j) for i in range(n) for j in range(i, n)]


def masked(ref, count):
    rows = lax.broadcasted_iota(jnp.int32, ref.shape, 0)
    return jnp.where(rows < count, ref[...], 0.0)


def products_kernel(scalars, basis_ref, block_ref, keep_ref, send_ref, all_ref, *, weight):
    count, core = scalars[0], scalars[1]
    basis = masked(basis_ref, count)
    block = masked(block_ref, count)
    turned = split(jnp.transpose(basis * weight))
    basis = split(basis)
    block = split(block)
    m, k = basis_ref.shape[1] // BLOCK, block_ref.shape[1] // BLOCK
    half_size = keep_ref.shape[0]
    position = 0
    for i in range(m):
        left = rows_of(turned, i * BLOCK, (i + 1) * BLOCK)
        own = dot3(left, columns_of(basis, i * BLOCK, m * BLOCK))
        cross = dot3(left, block)
        rest = jnp.dot(
            left[1],
            basis[1][:, i * BLOCK : (i + 1) * BLOCK],
            preferred_element_type=jnp.float32,
        )
        tiles = [own[:, j * BLOCK : (j + 1) * BLOCK] for j in range(m - i)]
        tiles[0] = tiles[0] + rest
        tiles += [cross[:, j * BLOCK : (j + 1) * BLOCK] for j in range(k)]
        for tile in tiles:
            all_ref[position] = tile
            position += 1
    keep_ref[...] = all_ref[pl.ds(core * half_size, half_size)]
    send_ref[...] = all_ref[pl.ds((1 - core) * half_size, half_size)]


def residual_kernel(
    scalars, own_ref, other_ref, basis_ref, block_ref, residual_ref, keep_ref, send_ref,
    s_hi, s_lo, gram_ref, *, weight
):
    count, core = scalars[0], scalars[1]
    m, k = basis_ref.shape[1] // BLOCK, block_ref.shape[1] // BLOCK
    half_size = own_ref.shape[0]
    first = core == 0

    def tile_at(position):
        mine, theirs = own_ref[position % half_size], other_ref[position % half_size]
        swap = first if position < half_size else jnp.logical_not(first)
        return jnp.where(swap, mine, theirs)

    position = 0
    coeffs = []
    eye = identity(BLOCK)
    for i in range(m):
        for j in range(i, m):
            tile = -tile_at(position)
            position += 1
            if i == j:
                tile = eye + tile
            hi, lo = split(tile)
            s_hi[i * BLOCK : (i + 1) * BLOCK, j * BLOCK : (j + 1) * BLOCK] = hi
            s_lo[i * BLOCK : (i + 1) * BLOCK, j * BLOCK : (j + 1) * BLOCK] = lo
            if i != j:
                hi, lo = split(jnp.transpose(tile))
                s_hi[j * BLOCK : (j + 1) * BLOCK, i * BLOCK : (i + 1) * BLOCK] = hi
                s_lo[j * BLOCK : (j + 1) * BLOCK, i * BLOCK : (i + 1) * BLOCK] = lo
        row = []
        for j in range(k):
            row.append(tile_at(position))
            position += 1
        coeffs.append(jnp.concatenate(row, axis=1))
    coeffs = jnp.concatenate(coeffs, axis=0)
    total = coeffs + dot3((s_hi[...], s_lo[...]), split(coeffs))
    basis = masked(basis_ref, count)
    residual = masked(block_ref, count) - jnp.dot(
        basis, total, precision=HIGHEST, preferred_element_type=jnp.float32
    )
    residual_ref[...] = residual
    turned = split(jnp.transpose(residual * weight))
    residual = split(residual)
    half_size = keep_ref.shape[0]
    position = 0
    for i in range(k):
        row = dot3(
            rows_of(turned, i * BLOCK, (i + 1) * BLOCK), columns_of(residual, i * BLOCK, k * BLOCK)
        )
        for j in range(k - i):
            gram_ref[position] = row[:, j * BLOCK : (j + 1) * BLOCK]
            position += 1
    keep_ref[...] = gram_ref[pl.ds(core * half_size, half_size)]
    send_ref[...] = gram_ref[pl.ds((1 - core) * half_size, half_size)]


def dot3_nt(a, b):
    ah, al = a
    bh, bl = b

    def one(p, q):
        return lax.dot_general(p, q, (((1,), (1,)), ((), ())), preferred_element_type=jnp.float32)

    return one(ah, bh) + (one(ah, bl) + one(al, bh))


def factor_kernel(scalars, own_ref, other_ref, residual_ref, new_ref, factor_ref, w, inv_ref):
    size = residual_ref.shape[1]
    first = scalars[1] == 0
    half_size = own_ref.shape[0]
    zero = jnp.zeros((BLOCK, BLOCK), jnp.float32)
    for position, (i, j) in enumerate(upper_pairs(size // BLOCK)):
        swap = first if position < half_size else jnp.logical_not(first)
        w[i * BLOCK : (i + 1) * BLOCK, j * BLOCK : (j + 1) * BLOCK] = jnp.where(
            swap, own_ref[position % half_size], other_ref[position % half_size]
        )
        if i != j:
            w[j * BLOCK : (j + 1) * BLOCK, i * BLOCK : (i + 1) * BLOCK] = zero
    residual = split(residual_ref[...])
    zero = jnp.zeros((STEP, BLOCK), jnp.float32)
    lane = lax.broadcasted_iota(jnp.int32, (PANEL, BLOCK), 1)
    row = lax.broadcasted_iota(jnp.int32, (PANEL, BLOCK), 0)
    lanes = lax.broadcasted_iota(jnp.int32, (STEP, BLOCK), 1)
    rows = lax.broadcasted_iota(jnp.int32, (STEP, BLOCK), 0)
    following = None
    for k in range(size // STEP):
        o = k * STEP
        end = o + STEP
        lo = o // BLOCK * BLOCK
        hi = lo + BLOCK
        a0 = o - lo
        e0 = STEP - a0
        square = w[o:end, lo:hi] if following is None else following
        v = []
        for q in range(STEP // PANEL):
            eye = (lane - e0 == row + PANEL * q).astype(jnp.float32)
            inside = (lane >= a0) & (lane < a0 + STEP)
            v.append(jnp.where(inside, square[PANEL * q : PANEL * q + PANEL, :], eye))
        d = jnp.concatenate(eliminate(v, a0), axis=0)
        swapped = pltpu.roll(d, STEP, 1)
        here = (lanes >= a0) & (lanes < a0 + STEP)
        left4 = twice_left(jnp.where(here, swapped, d))
        if end < size:
            lo2 = end // BLOCK * BLOCK
            part = stacked_dot(left4, w[o:end, lo2 : lo2 + BLOCK])
            drop = stacked_dot_tn(part, part)[end - lo2 : end - lo2 + STEP, :]
            following = w[end : end + STEP, lo2 : lo2 + BLOCK] - drop
        z = stacked_dot(left4, w[o:end, :])
        z_here = z[:, lo:hi]
        upper = jnp.where(
            here & (lanes - a0 >= rows), d, jnp.where(lanes >= a0 + STEP, z_here, 0.0)
        )
        lower = jnp.where(
            here, jnp.where(lanes - a0 <= rows, swapped, 0.0), jnp.where(lanes < a0, z_here, 0.0)
        )
        for c in range(0, size, BLOCK):
            band = slice(c, c + BLOCK)
            factor_ref[o:end, band] = zero if c < lo else (upper if c == lo else z[:, band])
            inv_ref[o:end, band] = z[:, band] if c < lo else (lower if c == lo else zero)
        if end < size:
            pieces = [z[:, :lo]] if lo else []
            pieces.append(jnp.where(here, swapped, z_here))
            if hi < size:
                pieces.append(z[:, hi:])
            first_lane = end // BLOCK * BLOCK
            drop = stacked_dot_tn(z[:, first_lane:], jnp.concatenate(pieces, axis=1))
            column = lax.broadcasted_iota(jnp.int32, (size - end, size), 1)
            w[end:size, :] = (
                jnp.where((column >= o) & (column < end), 0.0, w[end:size, :])
                - drop[end - first_lane :, :]
            )
        if end == hi:
            new_ref[:, lo:hi] = dot3_nt(
                columns_of(residual, 0, hi), split(inv_ref[lo:hi, 0:hi])
            )


def call(kernel, out_shapes, scratch, name):
    def run(scalars, *arrays):
        vmem = pl.BlockSpec(memory_space=pltpu.VMEM)
        return pl.pallas_call(
            kernel,
            out_shape=[jax.ShapeDtypeStruct(s, jnp.float32) for s in out_shapes],
            in_specs=[pl.BlockSpec(memory_space=pltpu.SMEM)] + [vmem] * len(arrays),
            out_specs=[vmem] * len(out_shapes),
            scratch_shapes=scratch,
            compiler_params=pltpu.CompilerParams(vmem_limit_bytes=24 << 20),
            name=name,
        )(scalars, *arrays)

    return run


def swap_cores(x):
    return lax.ppermute(x, "row_2", [(0, 1), (1, 0)])


def exchange(x, axes):
    return lax.all_to_all(x, axes, 0, 0, tiled=True)


def to_all(x, axes):
    count = lax.axis_size(axes)
    return exchange(jnp.broadcast_to(x[None], (count, *x.shape)), axes)


def direct_sum(part, axis):
    count = lax.axis_size(axis)
    parts = [
        lax.ppermute(part, axis, [(i, (i + d) % count) for i in range(count)])
        for d in range(1, count)
    ]
    return part + sum(parts[1:], parts[0])


def sum_halves(keep, send, near, far, direct):
    total = (keep + swap_cores(send)).reshape(lax.axis_size(near), -1, 8, 128)
    part = jnp.sum(exchange(total, near), axis=0)
    part = direct_sum(part, far) if direct else jnp.sum(to_all(part, far), axis=0)
    whole = to_all(part, near).reshape(keep.shape)
    return whole, swap_cores(whole)


def body(basis, block, counts):
    row_slots, size = block.shape
    m, k = basis.shape[1] // BLOCK, size // BLOCK
    devices = lax.axis_size(GRP) * lax.axis_size(ROW)
    weight = 1.0 / (row_slots * devices)
    scalars = jnp.stack([counts[0, 0], lax.axis_index("row_2").astype(jnp.int32)])
    tiles = (m * (m + 1) // 2 + m * k) // 2
    gram_tiles = k * (k + 1) // 4
    half = (tiles, BLOCK, BLOCK)
    gram_half = (gram_tiles, BLOCK, BLOCK)
    keep, send = call(
        functools.partial(products_kernel, weight=weight), [half, half],
        [pltpu.VMEM((2 * tiles, BLOCK, BLOCK), jnp.float32)], "products"
    )(scalars, basis, block)
    own, other = sum_halves(keep, send, SLAB, "grp_0", True)
    wide = pltpu.VMEM((m * BLOCK, m * BLOCK), jnp.bfloat16)
    residual, keep, send = call(
        functools.partial(residual_kernel, weight=weight),
        [block.shape, gram_half, gram_half],
        [wide, wide, pltpu.VMEM((2 * gram_tiles, BLOCK, BLOCK), jnp.float32)],
        "residual",
    )(scalars, own, other, basis, block)
    own, other = sum_halves(keep, send, PLANE, GRP, False)
    new_block, factor = call(
        factor_kernel,
        [block.shape, (size, size)],
        [
            pltpu.VMEM((size, size), jnp.float32),
            pltpu.VMEM((size, size), jnp.float32),
        ],
        "factor",
    )(scalars, own, other, residual)
    return new_block, factor


def solution(mesh):
    torus = Mesh(mesh.devices.reshape(mesh.shape["grp"] // 2, 2, 4, 4, 2), GRP_ROW)
    in_specs = (P(GRP_ROW, None), P(GRP_ROW, None), P(GRP, ROW))
    out_specs = (P(GRP_ROW, None), P())
    return jax.shard_map(body, mesh=torus, in_specs=in_specs, out_specs=out_specs, check_vma=False)
```
